512 devices in a mesh: ctx: 32 (over z, y_hi, core), head: 16 (over x, y_lo).
Axes of the slice: x: 4, y: 8 (y_hi: 2, y_lo: 4; y = y_hi * 4 + y_lo), z: 8, core: 2. Of those that a mesh axis runs over, the one named last changes fastest.
Arguments:
- features: bfloat16 [16384, 5376], P('ctx', 'head'), may hold values from -30 to 30
- query_weight: bfloat16 [5376, 4096], P('ctx', 'head'), as said below
- key_weight: bfloat16 [5376, 2048], P('ctx', 'head'), as said below
- value_weight: bfloat16 [5376, 2048], P('ctx', 'head'), may hold values from -0.078125 to 0.078125
- doc_lengths: int32 [8], replicated, may hold values from 1 to 8192, 16384 in all
- out_grad: bfloat16 [16384, 4096], P('ctx', 'head'), may hold values from -6 to 6
Outputs:
- attention: bfloat16 [16384, 4096], P('ctx', 'head')
- key_weight_grad: bfloat16 [5376, 2048], P('ctx', 'head')
- value_weight_grad: bfloat16 [5376, 2048], P('ctx', 'head')
The draws below stay inside these ranges and needn't reach their ends.
Inputs may be any that keep to these rules, and one draw needn't show every extreme that they name: `doc_lengths`: the lengths sum to 16384; the longest document holds half of them. `query_weight`: projection entries. `key_weight`: projection entries.
All inputs are finite; a program needn't handle non-finite values.
Results may differ from the reference program's by a relative error of at most 0.029.
Values may be sent and summed in bfloat16 or wider, within the bound.
No kernel may reach another device: no remote copies, remote signals or barrier semaphores. Data moves between devices by JAX's collectives and lax.ppermute only.
A program may use at most 64 MiB of HBM per device.

```python
import math
import jax
import jax.numpy as jnp
import numpy as np
from jax import lax

D = 5376
HEADS_Q = 32
HEADS_KV = 16
HEAD_DIM = 128
WINDOW = 1024
TOK_DEV = 512
SPAN = 2
TOKENS = 16384
DOCS = 8
N_CTX = 32


def query_base(key):
    raw = jnp.clip(jax.random.normal(jax.random.fold_in(key, 11), (D, HEADS_Q * HEAD_DIM), jnp.float32), -6.0, 6.0)
    return raw / jnp.sqrt(jnp.float32(D))


def draw_query_weight(key, part):
    return query_base(key).astype(jnp.bfloat16)


def draw_key_weight(key, part):
    noise = jnp.clip(jax.random.normal(jax.random.fold_in(key, 12), (D, HEADS_KV * HEAD_DIM), jnp.float32), -6.0, 6.0) / jnp.sqrt(jnp.float32(D))
    return noise.astype(jnp.bfloat16)


def draw_features(key, part):
    return jnp.clip(jax.random.normal(jax.random.fold_in(key, 1), (TOKENS, D), jnp.float32), -6.0, 6.0).astype(jnp.bfloat16)


def shard_levels(own_key, extent, cuts, low, top_value):
    gain = 1.0
    for axis_at, blocks in cuts:
        heights = jax.random.uniform(jax.random.fold_in(jax.random.fold_in(own_key, 6), axis_at), (blocks,), jnp.float32, low / len(cuts), top_value / len(cuts))
        gain = gain * jnp.repeat(jnp.exp(heights), extent[axis_at] // blocks).reshape((-1,) + (1,) * (len(extent) - 1 - axis_at))
    return gain


def profile(number_of, total, reach, skew):
    loads = [(1 << 20) // math.isqrt(standing ** skew) + 1 for standing in range(2, number_of + 1)]
    surplus, given = total - reach - (number_of - 1), [1] * (number_of - 1)
    while surplus > 0:
        free = [i for i in range(number_of - 1) if given[i] < reach]
        mass, remaining = sum([loads[i] for i in free]), surplus
        for i in free:
            more = min(reach - given[i], max(1, remaining * loads[i] // mass), surplus)
            given[i] = given[i] + more
            surplus = surplus - more
    return np.array([reach] + given)


def uneven_parts(key, amount, total, bound, skew):
    if amount == 2:
        one = jax.random.randint(key, (), max(1, total - bound), min(bound, total - 1) + 1)
        return jnp.stack([one, total - one])
    tallies = jnp.asarray(profile(amount, total, bound, skew), jnp.int32)
    couples = (amount - 1) // 2
    source_of, receiver = tallies[1:1 + 2 * couples:2], tallies[2:2 + 2 * couples:2]
    slack = jnp.minimum(source_of - 1, bound - receiver)
    passed = jax.random.randint(jax.random.fold_in(key, 1), (couples,), 0, 1 << 20) % (slack + 1)
    tallies = tallies.at[1:1 + 2 * couples:2].set(source_of - passed).at[2:2 + 2 * couples:2].set(receiver + passed)
    return tallies[jax.random.permutation(jax.random.fold_in(key, 2), amount)]


def normal_values(rng, dims, spread, most, split=(), kind=jnp.bfloat16):
    values = spread * jax.random.normal(rng, dims, jnp.float32)
    if split:
        values = values * shard_levels(rng, dims, split, -0.22, 0.18)
    return jnp.clip(values, -most, most).astype(kind)


def setup_inputs(seed: int = 0) -> dict:
    splits = jax.random.split(jax.random.key(seed), 7)
    return {
        "features": draw_features(jax.random.fold_in(splits[6], 71), 0),
        "query_weight": draw_query_weight(jax.random.fold_in(splits[6], 71), 0),
        "key_weight": draw_key_weight(jax.random.fold_in(splits[6], 71), 0),
        "value_weight": normal_values(splits[3], (D, HEADS_KV * HEAD_DIM), D ** -0.5, 0.078125, ((0, 32), (1, 16))),
        "doc_lengths": uneven_parts(splits[4], DOCS, TOKENS, TOKENS // 2, 2).astype(jnp.int32),
        "out_grad": normal_values(splits[5], (TOKENS, HEADS_Q * HEAD_DIM), 1.0, 6.0, ((0, 32), (1, 16))),
    }


ROPE_BASE = 10000.0


def rotate_half(values):
    middle = values.shape[-1] // 2
    return jnp.concatenate([-values[..., middle:], values[..., :middle]], axis=-1)


def rope_tables(offsets):
    middle = HEAD_DIM // 2
    inverse = ROPE_BASE ** (-(jnp.arange(middle).astype(jnp.float32) * 2.0 / HEAD_DIM))
    angles = offsets.astype(jnp.float32)[:, None] * inverse[None, :]
    cosine = jnp.cos(angles)
    sine_table = jnp.sin(angles)
    return jnp.concatenate([cosine, cosine], axis=-1), jnp.concatenate([sine_table, sine_table], axis=-1)


def rotate(values, cosine, sine_table):
    return values * cosine[:, None, :] + rotate_half(values) * sine_table[:, None, :]


def unrotate(values, cosine, sine_table):
    return values * cosine[:, None, :] - rotate_half(values) * sine_table[:, None, :]


def start_of(positions, starts):
    candidates = jnp.where(starts[None, :] <= positions[:, None], starts[None, :], -1)
    return jnp.max(candidates, axis=1).astype(jnp.int32)


def rounded(values):
    return lax.optimization_barrier(values.astype(jnp.bfloat16)).astype(jnp.float32)


def reference(features, query_weight, key_weight, value_weight, doc_lengths, out_grad):
    highest = lax.Precision.HIGHEST
    query_scale = (D / HEADS_Q) ** -0.5
    group_size = HEADS_Q // HEADS_KV
    starts = (jnp.cumsum(doc_lengths) - doc_lengths).astype(jnp.int32)
    token_index = jnp.arange(TOKENS, dtype=jnp.int32)
    token_start = start_of(token_index, starts)
    cosine, sine_table = rope_tables(token_index - token_start)
    query_proj = jnp.dot(features, query_weight, preferred_element_type=jnp.float32).reshape(TOKENS, HEADS_Q, HEAD_DIM)
    key_proj = jnp.dot(features, key_weight, preferred_element_type=jnp.float32).reshape(TOKENS, HEADS_KV, HEAD_DIM)
    value_proj = jnp.dot(features, value_weight, preferred_element_type=jnp.float32).reshape(TOKENS, HEADS_KV, HEAD_DIM)
    queries = (rotate(query_proj, cosine, sine_table) * query_scale).astype(jnp.bfloat16)
    keys_all = rotate(key_proj, cosine, sine_table).astype(jnp.bfloat16)
    values_all = value_proj.astype(jnp.bfloat16)
    pad_rows = SPAN * TOK_DEV
    key_rows = (SPAN + 1) * TOK_DEV
    zero_rows = jnp.zeros((pad_rows, HEADS_KV, HEAD_DIM), jnp.bfloat16)
    keys_pad = jnp.concatenate([zero_rows, keys_all], axis=0)
    values_pad = jnp.concatenate([zero_rows, values_all], axis=0)
    start_pad = jnp.concatenate([jnp.full((pad_rows,), -1, jnp.int32), token_start], axis=0)
    grouped_all = queries.reshape(TOKENS, HEADS_KV, group_size, HEAD_DIM)
    grads_all = out_grad.reshape(TOKENS, HEADS_KV, group_size, HEAD_DIM)

    def block_step(running, block_index):
        key_acc, value_acc = running
        first_row = (block_index * TOK_DEV).astype(jnp.int32)
        grouped = lax.dynamic_slice_in_dim(grouped_all, first_row, TOK_DEV, 0)
        grad_heads = lax.dynamic_slice_in_dim(grads_all, first_row, TOK_DEV, 0)
        key_block = lax.dynamic_slice_in_dim(keys_pad, first_row, key_rows, 0)
        value_block = lax.dynamic_slice_in_dim(values_pad, first_row, key_rows, 0)
        query_start = lax.dynamic_slice_in_dim(token_start, first_row, TOK_DEV, 0)
        key_start = lax.dynamic_slice_in_dim(start_pad, first_row, key_rows, 0)
        query_index = first_row + jnp.arange(TOK_DEV, dtype=jnp.int32)
        key_index = first_row - pad_rows + jnp.arange(key_rows, dtype=jnp.int32)
        offsets_qk = query_index[:, None] - key_index[None, :]
        allowed = (key_index[None, :] >= 0) & (offsets_qk >= 0) & (offsets_qk < WINDOW) & (query_start[:, None] == key_start[None, :])
        scores = jnp.einsum("tkgd,skd->kgts", grouped.astype(jnp.float32), key_block.astype(jnp.float32), precision=highest)
        row_max = jnp.max(jnp.where(allowed, scores, -jnp.inf), axis=-1, keepdims=True)
        raw_weights = jnp.where(allowed, jnp.exp(scores - row_max), 0.0)
        prob_soft = raw_weights / jnp.sum(raw_weights, axis=-1, keepdims=True)
        probs_low = prob_soft.astype(jnp.bfloat16)
        attended = jnp.einsum("kgts,skd->tkgd", probs_low.astype(jnp.float32), value_block.astype(jnp.float32), precision=highest).astype(jnp.bfloat16)
        out_dot = jnp.einsum("tkgd,tkgd->kgt", grad_heads.astype(jnp.float32), attended.astype(jnp.float32), precision=highest)[..., None]
        value_partial = jnp.einsum("kgts,tkgd->skd", probs_low.astype(jnp.float32), grad_heads.astype(jnp.float32), precision=highest)
        prob_grad = jnp.einsum("tkgd,skd->kgts", grad_heads.astype(jnp.float32), value_block.astype(jnp.float32), precision=highest)
        score_grad = (prob_soft * (prob_grad - out_dot)).astype(jnp.bfloat16)
        key_partial = jnp.einsum("kgts,tkgd->skd", score_grad.astype(jnp.float32), grouped.astype(jnp.float32), precision=highest)
        key_acc = lax.dynamic_update_slice_in_dim(key_acc, lax.dynamic_slice_in_dim(key_acc, first_row, key_rows, 0) + key_partial, first_row, 0)
        value_acc = lax.dynamic_update_slice_in_dim(value_acc, lax.dynamic_slice_in_dim(value_acc, first_row, key_rows, 0) + value_partial, first_row, 0)
        return (key_acc, value_acc), attended

    empty_acc = jnp.zeros((pad_rows + TOKENS, HEADS_KV, HEAD_DIM), jnp.float32)
    (key_acc, value_acc), attended_all = lax.scan(block_step, (empty_acc, empty_acc), jnp.arange(N_CTX, dtype=jnp.int32))
    attention = attended_all.reshape(TOKENS, HEADS_Q * HEAD_DIM)
    key_grad = unrotate(key_acc[pad_rows:], cosine, sine_table).astype(jnp.bfloat16).reshape(TOKENS, HEADS_KV * HEAD_DIM)
    value_grad = value_acc[pad_rows:].astype(jnp.bfloat16).reshape(TOKENS, HEADS_KV * HEAD_DIM)
    pair_grads = jnp.concatenate([key_grad, value_grad], axis=1)

    def token_step(running, block_index):
        first_row = (block_index * TOK_DEV).astype(jnp.int32)
        feature_rows = lax.dynamic_slice_in_dim(features, first_row, TOK_DEV, 0)
        grad_rows = lax.dynamic_slice_in_dim(pair_grads, first_row, TOK_DEV, 0)
        term = jnp.dot(feature_rows.T, grad_rows, preferred_element_type=jnp.float32)
        return running + rounded(term), None

    weight_sum, unused_blocks = lax.scan(token_step, jnp.zeros((D, 2 * HEADS_KV * HEAD_DIM), jnp.float32), jnp.arange(N_CTX, dtype=jnp.int32))
    kv_width = HEADS_KV * HEAD_DIM
    return (attention, weight_sum[:, :kv_width].astype(jnp.bfloat16), weight_sum[:, kv_width:].astype(jnp.bfloat16))
```

```python
import functools

import jax
import jax.numpy as jnp
from jax import lax
from jax.experimental import pallas as pl
from jax.experimental.pallas import tpu as pltpu
from jax.sharding import Mesh
from jax.sharding import PartitionSpec as P

HEADS_Q = 32
HEAD_DIM = 128
WINDOW = 1024
SPAN = 2
HEAD = ("x", "y")
CORES = 2
HIGH = 2
ROPE_BASE = 10000.0


def cycled(value, axis, step):
    count = lax.axis_size(axis)
    return lax.ppermute(value, axis, [(i, (i + step) % count) for i in range(count)])


def core_swapped(value):
    count = lax.axis_size("ctx")
    return lax.ppermute(value, "ctx", [(i, i ^ 1) for i in range(count)])


def passed_along(block, distance):
    devices = range(lax.axis_size("ctx"))
    route = [(i - distance, i) for i in devices if i - distance in devices]
    return lax.ppermute(block, "ctx", route)


def rotate_half(values):
    middle = values.shape[-1] // 2
    return jnp.concatenate([-values[..., middle:], values[..., :middle]], axis=-1)


def rope_tables(offsets):
    middle = HEAD_DIM // 2
    inverse = ROPE_BASE ** (-(jnp.arange(middle).astype(jnp.float32) * 2.0 / HEAD_DIM))
    angles = offsets.astype(jnp.float32)[:, None] * inverse[None, :]
    cosine = jnp.cos(angles)
    sine_table = jnp.sin(angles)
    return (
        jnp.concatenate([cosine, cosine], axis=-1),
        jnp.concatenate([sine_table, sine_table], axis=-1),
    )


def rotate(values, cosine, sine_table):
    return values * cosine[:, None, :] + rotate_half(values) * sine_table[:, None, :]


def unrotate(values, cosine, sine_table):
    return values * cosine[:, None, :] - rotate_half(values) * sine_table[:, None, :]


def start_of(positions, starts):
    candidates = jnp.where(starts[None, :] <= positions[:, None], starts[None, :], -1)
    return jnp.max(candidates, axis=1)


def spread_features(own):
    rows = own.shape[0]
    half = -(-(rows // 2) // 16) * 16
    above, below = cycled(own, "y", 1), cycled(own, "y", -1)
    across = cycled(own, "y", 2)
    batches = [
        (own, [(0, 0)]),
        (jnp.concatenate([above, below]), [(3, 0), (1, rows)]),
        (across, [(2, 0)]),
    ]
    arrays, pieces = [], []

    def add(array, x_step, entries):
        for y_step, at, count, slab_at in entries:
            pieces.append((len(arrays), at, count, x_step, y_step, slab_at))
        arrays.append(array)

    for batch, slabs in batches:
        cut = half if len(slabs) == 1 else rows
        left, right = cycled(batch, "x", 1), cycled(batch, "x", -1)
        far_top, far_low = cycled(left[:cut], "x", 1), cycled(right[cut:], "x", -1)
        whole = [(y_step, at, rows, 0) for y_step, at in slabs]
        add(batch, 0, whole)
        add(left, 3, whole)
        add(right, 1, whole)
        if len(slabs) == 1:
            add(far_top, 2, [(slabs[0][0], 0, cut, 0)])
            add(far_low, 2, [(slabs[0][0], 0, rows - cut, cut)])
        else:
            add(far_top, 2, [(slabs[0][0], 0, rows, 0)])
            add(far_low, 2, [(slabs[1][0], 0, rows, 0)])
    return arrays, pieces


CONTRACT_ROWS = (((0,), (0,)), ((), ()))


def project_kernel(pieces, columns, place_ref, weights_ref, *refs):
    out_ref = refs[-1]
    first, last = columns
    for number, (array, at, count, x_step, y_step, slab_at) in enumerate(pieces):
        weight = weights_ref[place_ref[x_step * 4 + y_step], slab_at : slab_at + count, first:last]
        term = lax.dot_general(
            refs[array][at : at + count],
            weight,
            CONTRACT_ROWS,
            preferred_element_type=jnp.float32,
        )
        out_ref[...] = term if number == 0 else out_ref[...] + term


def project(arrays, pieces, place, weights, columns):
    tokens = arrays[0].shape[1]
    width = columns[1] - columns[0]
    vmem = pl.BlockSpec(memory_space=pltpu.VMEM)
    depth = sum(piece[2] for piece in pieces)
    return pl.pallas_call(
        functools.partial(project_kernel, pieces, columns),
        out_shape=jax.ShapeDtypeStruct((tokens, width), jnp.float32),
        in_specs=[pl.BlockSpec(memory_space=pltpu.SMEM)] + [vmem] * (1 + len(arrays)),
        out_specs=vmem,
        compiler_params=pltpu.CompilerParams(vmem_limit_bytes=40 << 20),
        cost_estimate=pl.CostEstimate(
            flops=2 * tokens * depth * width,
            bytes_accessed=2 * depth * (tokens + width) + 4 * tokens * width,
            transcendentals=0,
        ),
        name="project",
    )(place, weights, *arrays)


def weight_grad_kernel(pieces, place_ref, grads_ref, *refs):
    out_ref = refs[-1]
    for array, at, count, x_step, y_step, slab_at in pieces:
        term = jnp.dot(
            refs[array][at : at + count], grads_ref[...], preferred_element_type=jnp.float32
        )
        out_ref[place_ref[x_step * 4 + y_step], slab_at : slab_at + count] = term.astype(
            jnp.bfloat16
        )


def weight_grad(arrays, pieces, place, grads, rows):
    width = grads.shape[1]
    tokens = grads.shape[0]
    vmem = pl.BlockSpec(memory_space=pltpu.VMEM)
    depth = sum(piece[2] for piece in pieces)
    return pl.pallas_call(
        functools.partial(weight_grad_kernel, pieces),
        out_shape=jax.ShapeDtypeStruct((16, rows, width), jnp.bfloat16),
        in_specs=[pl.BlockSpec(memory_space=pltpu.SMEM)] + [vmem] * (1 + len(arrays)),
        out_specs=vmem,
        compiler_params=pltpu.CompilerParams(vmem_limit_bytes=40 << 20),
        cost_estimate=pl.CostEstimate(
            flops=2 * tokens * depth * width,
            bytes_accessed=2 * depth * (tokens + width) + 2 * tokens * width,
            transcendentals=0,
        ),
        name="weight_grad",
    )(place, grads, *arrays)


def scattered_sum(terms):
    core = lax.axis_index("ctx") % CORES
    kept = jnp.where(core == 0, terms[:, 0], terms[:, 1])
    sent = jnp.where(core == 0, terms[:, 1], terms[:, 0])
    chip = (kept.astype(jnp.float32) + core_swapped(sent).astype(jnp.float32)).astype(jnp.bfloat16)
    count = lax.axis_size("ctx")
    groups = [[i for i in range(count) if i % CORES == c] for c in range(CORES)]
    landed = lax.all_to_all(chip, "ctx", 0, 0, axis_index_groups=groups, tiled=True)
    return jnp.sum(landed.astype(jnp.float32), axis=0)


def shards(features, query_weight, key_weight, value_weight, doc_lengths, out_grad):
    tok_rows, slab_rows = features.shape
    query_cols = query_weight.shape[1]
    value_cols = key_weight.shape[1]
    query_heads = query_cols // HEAD_DIM
    value_heads = value_cols // HEAD_DIM
    group_size = query_heads // value_heads
    model_width = slab_rows * 16
    query_scale = (model_width / HEADS_Q) ** (-0.5)
    ctx_index = lax.axis_index("ctx")

    packed = jnp.concatenate([query_weight, key_weight, value_weight], axis=1)
    weights = lax.all_gather(packed, "ctx", axis=0, tiled=True).reshape(16, slab_rows, -1)
    arrays, pieces = spread_features(features.T)
    x_at, y_at = lax.axis_index("x"), lax.axis_index("y")
    step = jnp.arange(4, dtype=jnp.int32)
    place = (((x_at + step) % 4)[:, None] * 4 + ((y_at + step) % 4)[None, :]).reshape(16)
    place = place.astype(jnp.int32)

    kv_proj = project(arrays, pieces, place, weights, (query_cols, query_cols + 2 * value_cols))
    starts = jnp.cumsum(doc_lengths) - doc_lengths
    query_index = ctx_index * tok_rows + jnp.arange(tok_rows, dtype=jnp.int32)
    query_start = start_of(query_index, starts)
    cosine, sine_table = rope_tables(query_index - query_start)
    own_keys = rotate(
        kv_proj[:, :value_cols].reshape(tok_rows, value_heads, HEAD_DIM), cosine, sine_table
    ).astype(jnp.bfloat16)
    own_values = kv_proj[:, value_cols:].reshape(tok_rows, value_heads, HEAD_DIM)
    own_values = own_values.astype(jnp.bfloat16)
    key_value = jnp.stack([own_keys, own_values])
    earlier = [passed_along(key_value, distance) for distance in range(SPAN, 0, -1)]
    query_proj = project(arrays, pieces, place, weights, (0, query_cols))
    queries = (
        rotate(query_proj.reshape(tok_rows, query_heads, HEAD_DIM), cosine, sine_table)
        * query_scale
    ).astype(jnp.bfloat16)
    key_block = jnp.concatenate(earlier + [key_value], axis=1)
    key_rows = key_block.shape[1]
    key_index = (ctx_index - SPAN) * tok_rows + jnp.arange(key_rows, dtype=jnp.int32)
    key_start = start_of(key_index, starts)
    offsets_qk = query_index[:, None] - key_index[None, :]
    allowed = (
        (key_index[None, :] >= 0)
        & (offsets_qk >= 0)
        & (offsets_qk < SPAN * tok_rows)
        & (query_start[:, None] == key_start[None, :])
    )
    grouped = queries.reshape(tok_rows, value_heads, group_size, HEAD_DIM)
    scores = jnp.einsum("tkgd,skd->kgts", grouped, key_block[0], preferred_element_type=jnp.float32)
    row_max = jnp.max(jnp.where(allowed, scores, -jnp.inf), axis=-1, keepdims=True)
    raw_weights = jnp.where(allowed, jnp.exp(scores - row_max), 0.0)
    prob_soft = raw_weights / jnp.sum(raw_weights, axis=-1, keepdims=True)
    probs_low = prob_soft.astype(jnp.bfloat16)
    attended = jnp.einsum(
        "kgts,skd->tkgd", probs_low, key_block[1], preferred_element_type=jnp.float32
    ).astype(jnp.bfloat16)
    attention = attended.reshape(tok_rows, query_cols)
    grad_heads = out_grad.reshape(tok_rows, value_heads, group_size, HEAD_DIM)
    out_dot = jnp.sum(
        grad_heads.astype(jnp.float32) * attended.astype(jnp.float32), axis=-1
    ).transpose(1, 2, 0)[..., None]
    value_partial = jnp.einsum(
        "kgts,tkgd->skd", probs_low, grad_heads, preferred_element_type=jnp.float32
    )
    prob_grad = jnp.einsum(
        "tkgd,skd->kgts", grad_heads, key_block[1], preferred_element_type=jnp.float32
    )
    score_grad = (prob_soft * (prob_grad - out_dot)).astype(jnp.bfloat16)
    key_partial = jnp.einsum(
        "kgts,tkgd->skd", score_grad, grouped, preferred_element_type=jnp.float32
    )
    partials = jnp.stack([key_partial, value_partial])

    def piece_of(distance):
        return partials[:, (SPAN - distance) * tok_rows : (SPAN - distance + 1) * tok_rows]

    returned = piece_of(0)
    for distance in range(1, SPAN + 1):
        returned = returned + passed_along(
            piece_of(distance).astype(jnp.bfloat16), -distance
        ).astype(jnp.float32)
    key_grad = (
        unrotate(returned[0], cosine, sine_table).astype(jnp.bfloat16).reshape(tok_rows, value_cols)
    )
    value_grad = returned[1].astype(jnp.bfloat16).reshape(tok_rows, value_cols)
    pair_grads = jnp.concatenate([key_grad, value_grad], axis=1)
    terms = weight_grad(arrays, pieces, place, pair_grads, slab_rows)
    weight_grads = scattered_sum(terms.reshape(16, CORES, slab_rows // CORES, -1))
    return (
        attention,
        weight_grads[:, :value_cols].astype(jnp.bfloat16),
        weight_grads[:, value_cols:].astype(jnp.bfloat16),
    )


def solution(mesh):
    torus = Mesh(mesh.devices.reshape(mesh.shape["ctx"], 4, 4), ("ctx", "x", "y"))
    placed = (P("ctx", HEAD), P("ctx", HEAD), P("ctx", HEAD), P("ctx", HEAD), P(), P("ctx", HEAD))
    return jax.shard_map(
        shards,
        mesh=torus,
        in_specs=placed,
        out_specs=(P("ctx", HEAD), P("ctx", HEAD), P("ctx", HEAD)),
        check_vma=False,
    )
```

```python
import functools

import jax
import jax.numpy as jnp
from jax import lax
from jax.experimental import pallas as pl
from jax.experimental.pallas import tpu as pltpu
from jax.sharding import Mesh
from jax.sharding import PartitionSpec as P

HEADS_Q = 32
HEAD_DIM = 128
WINDOW = 1024
SPAN = 2
CORES = 2
CTX = ("z", "far", "core")
HEAD = ("x", "y")
ROPE_BASE = 10000.0


def cycled(value, axis, step):
    count = lax.axis_size(axis)
    return lax.ppermute(value, axis, [(i, (i + step) % count) for i in range(count)])


def passed_along(block, distance):
    devices = range(lax.axis_size(CTX))
    route = [(i - distance, i) for i in devices if i - distance in devices]
    return lax.ppermute(block, CTX, route)


def rope_tables(offsets):
    middle = HEAD_DIM // 2
    inverse = ROPE_BASE ** (-(jnp.arange(middle).astype(jnp.float32) * 2.0 / HEAD_DIM))
    angles = offsets.astype(jnp.float32)[:, None] * inverse[None, :]
    cosine = jnp.cos(angles)
    sine = jnp.sin(angles)
    return (
        jnp.concatenate([cosine, cosine], axis=-1),
        jnp.concatenate([-sine, sine], axis=-1),
    )


def start_of(positions, starts):
    candidates = jnp.where(starts[None, :] <= positions[:, None], starts[None, :], -1)
    return jnp.max(candidates, axis=1)


def spread_features(own):
    arrays, pieces = [], []

    def add(array, entries):
        for at, (x_step, y_step, half) in enumerate(entries):
            pieces.append((len(arrays), at, x_step, y_step, half))
        arrays.append(array)

    def across(batch, y_steps):
        halves = [(y_step, half) for y_step in y_steps for half in range(2)]
        add(batch, [(0, *entry) for entry in halves])
        for x_step in (1, 3, 2):
            add(cycled(batch, "x", -x_step), [(x_step, *entry) for entry in halves])

    row = lax.all_gather(own, "x", axis=0, tiled=True)
    add(row, [(-1 - x_at, 0, half) for x_at in range(4) for half in range(2)])
    sides = jnp.concatenate([cycled(own, "y", 1), cycled(own, "y", -1)])
    own, sides = lax.optimization_barrier((own, sides))
    across(sides, (3, 1))
    across(cycled(own, "y", 2), (2,))
    return arrays, pieces, sides


def place_of(place_ref, x_step, y_step):
    if x_step < 0:
        return (-1 - x_step) * 4 + place_ref[17]
    return place_ref[x_step * 4 + y_step]


CONTRACT_ROWS = (((0,), (0,)), ((), ()))
CONTRACT_COLS = (((1,), (1,)), ((), ()))
BLOCK = 256


def turned(values, cosine, sine_signed):
    return values * cosine + pltpu.roll(values, HEAD_DIM // 2, 1) * sine_signed


def unturned(values, cosine, sine_signed):
    return values * cosine - pltpu.roll(values, HEAD_DIM // 2, 1) * sine_signed


def accumulated(pieces, columns, place_ref, weights_ref, arrays, total):
    first, last = columns
    for number, (array, at, x_step, y_step, half) in enumerate(pieces):
        place = place_of(place_ref, x_step, y_step)
        weight = weights_ref[(place // 2) * CORES + half, place % 2, :, first:last]
        term = lax.dot_general(
            arrays[array][at], weight, CONTRACT_ROWS, preferred_element_type=jnp.float32
        )
        total[...] = term if number == 0 else total[...] + term


def key_value_kernel(pieces, columns, place_ref, weights_ref, cos_ref, sin_ref, *refs):
    *arrays, out_ref, total = refs
    accumulated(pieces, columns, place_ref, weights_ref, arrays, total)
    keys = turned(total[:, :HEAD_DIM], cos_ref[...], sin_ref[...])
    out_ref[0] = keys.astype(jnp.bfloat16)
    out_ref[1] = total[:, HEAD_DIM:].astype(jnp.bfloat16)


def query_kernel(pieces, columns, place_ref, weights_ref, cos_ref, sin_ref, *refs, scale):
    *arrays, out_ref, total = refs
    accumulated(pieces, columns, place_ref, weights_ref, arrays, total)
    for head in range((columns[1] - columns[0]) // HEAD_DIM):
        part = total[:, head * HEAD_DIM : (head + 1) * HEAD_DIM]
        queries = turned(part, cos_ref[...], sin_ref[...]) * scale
        out_ref[:, head * HEAD_DIM : (head + 1) * HEAD_DIM] = queries.astype(jnp.bfloat16)


def attention_kernel(low_ref, q_ref, far_ref, near_ref, own_ref, grad_ref, att_ref, *refs):
    far_out, near_out, own_out, keys, values, acc = refs
    tokens, width = q_ref.shape
    for number, ref in enumerate((far_ref, near_ref, own_ref)):
        keys[number * tokens : (number + 1) * tokens] = ref[0]
        values[number * tokens : (number + 1) * tokens] = ref[1]
    acc[...] = jnp.zeros_like(acc)
    span = 2 * tokens + BLOCK
    heads = width // HEAD_DIM
    for head in range(heads):
        cols = slice(head * HEAD_DIM, (head + 1) * HEAD_DIM)
        for at in range(0, tokens, BLOCK):
            rows = slice(at, at + BLOCK)
            window = slice(at, at + span)
            low = low_ref[:, rows]
            key_at = lax.broadcasted_iota(jnp.int32, (span, BLOCK), 0) + at
            query_at = lax.broadcasted_iota(jnp.int32, (span, BLOCK), 1) + (2 * tokens + at)
            allowed = (key_at >= low) & (key_at <= query_at)
            query = q_ref[rows, cols]
            grad = grad_ref[rows, cols]
            scores = lax.dot_general(
                keys[window], query, CONTRACT_COLS, preferred_element_type=jnp.float32
            )
            scores = jnp.where(allowed, scores, -jnp.inf)
            raw = jnp.exp(scores - jnp.max(scores, axis=0, keepdims=True))
            probs = raw * (1.0 / jnp.sum(raw, axis=0, keepdims=True))
            low_probs = probs.astype(jnp.bfloat16)
            attended = lax.dot_general(
                values[window], low_probs, CONTRACT_ROWS, preferred_element_type=jnp.float32
            )
            attended = attended.T.astype(jnp.bfloat16)
            att_ref[rows, cols] = attended
            product = grad.astype(jnp.float32) * attended.astype(jnp.float32)
            out_dot = jnp.sum(product.T, axis=0, keepdims=True)
            acc[1, window] += jnp.dot(low_probs, grad, preferred_element_type=jnp.float32)
            prob_grad = lax.dot_general(
                values[window], grad, CONTRACT_COLS, preferred_element_type=jnp.float32
            )
            score_grad = (probs * (prob_grad - out_dot)).astype(jnp.bfloat16)
            acc[0, window] += jnp.dot(score_grad, query, preferred_element_type=jnp.float32)
    far_out[...] = acc[:, :tokens].astype(jnp.bfloat16)
    near_out[...] = acc[:, tokens : 2 * tokens].astype(jnp.bfloat16)
    own_out[...] = acc[:, 2 * tokens :]


def attention_call(low, queries, far, near, own, grads):
    tokens, width = queries.shape
    vmem = pl.BlockSpec(memory_space=pltpu.VMEM)
    block = jax.ShapeDtypeStruct(own.shape, jnp.bfloat16)
    pairs = tokens * (2 * tokens + BLOCK) * (width // HEAD_DIM)
    return pl.pallas_call(
        attention_kernel,
        out_shape=(
            jax.ShapeDtypeStruct((tokens, width), jnp.bfloat16),
            block,
            block,
            jax.ShapeDtypeStruct(own.shape, jnp.float32),
        ),
        in_specs=[vmem] * 6,
        out_specs=(vmem,) * 4,
        scratch_shapes=[
            pltpu.VMEM((3 * tokens, HEAD_DIM), jnp.bfloat16),
            pltpu.VMEM((3 * tokens, HEAD_DIM), jnp.bfloat16),
            pltpu.VMEM((2, 3 * tokens, HEAD_DIM), jnp.float32),
        ],
        compiler_params=pltpu.CompilerParams(vmem_limit_bytes=24 << 20),
        cost_estimate=pl.CostEstimate(
            flops=10 * pairs * HEAD_DIM,
            bytes_accessed=4 * tokens * width * 4,
            transcendentals=pairs,
        ),
        name="attention",
    )(low, queries, far, near, own, grads)


def project(kernel, out_shape, arrays, pieces, columns, place, weights, tables):
    tokens = arrays[0].shape[2]
    width = columns[1] - columns[0]
    depth = len(pieces) * arrays[0].shape[1]
    vmem = pl.BlockSpec(memory_space=pltpu.VMEM)
    return pl.pallas_call(
        functools.partial(kernel, pieces, columns),
        out_shape=out_shape,
        in_specs=[pl.BlockSpec(memory_space=pltpu.SMEM)] + [vmem] * (3 + len(arrays)),
        out_specs=vmem,
        scratch_shapes=[pltpu.VMEM((tokens, width), jnp.float32)],
        compiler_params=pltpu.CompilerParams(vmem_limit_bytes=24 << 20),
        cost_estimate=pl.CostEstimate(
            flops=2 * tokens * depth * width,
            bytes_accessed=2 * depth * (tokens + width) + 4 * tokens * width,
            transcendentals=0,
        ),
        name="project",
    )(place, weights, *tables, *arrays)


def weight_grad_kernel(pieces, place_ref, own_ref, near_ref, far_ref, cos_ref, sin_ref, *refs):
    *arrays, kept_ref, sent_ref = refs
    core = place_ref[16]
    sums = [
        own_ref[i] + near_ref[i].astype(jnp.float32) + far_ref[i].astype(jnp.float32)
        for i in range(2)
    ]
    key_grad = unturned(sums[0], cos_ref[...], sin_ref[...])
    grads = jnp.concatenate([key_grad, sums[1]], axis=1).astype(jnp.bfloat16)
    for array, at, x_step, y_step, half in pieces:
        term = jnp.dot(arrays[array][at], grads, preferred_element_type=jnp.float32)
        term = term.astype(jnp.bfloat16)
        place = place_of(place_ref, x_step, y_step)

        @pl.when(core == half)
        def _():
            kept_ref[place] = term

        @pl.when(core != half)
        def _():
            sent_ref[place] = term


def weight_grad(arrays, pieces, place, own, near, far, tables):
    rows, tokens = arrays[0].shape[1:]
    width = 2 * HEAD_DIM
    vmem = pl.BlockSpec(memory_space=pltpu.VMEM)
    depth = len(pieces) * rows
    block = jax.ShapeDtypeStruct((16, rows, width), jnp.bfloat16)
    return pl.pallas_call(
        functools.partial(weight_grad_kernel, pieces),
        out_shape=(block, block),
        in_specs=[pl.BlockSpec(memory_space=pltpu.SMEM)] + [vmem] * (5 + len(arrays)),
        out_specs=(vmem, vmem),
        compiler_params=pltpu.CompilerParams(vmem_limit_bytes=24 << 20),
        cost_estimate=pl.CostEstimate(
            flops=2 * tokens * depth * width,
            bytes_accessed=2 * depth * (tokens + width) + 2 * tokens * width,
            transcendentals=0,
        ),
        name="weight_grad",
    )(place, own, near, far, *tables, *arrays)


def scattered_sum(kept, sent):
    chip = kept.astype(jnp.float32) + cycled(sent, "core", 1).astype(jnp.float32)
    chip = chip.astype(jnp.bfloat16)
    landed = lax.all_to_all(chip, ("z", "far"), 0, 0, tiled=True)
    return jnp.sum(landed.astype(jnp.float32), axis=0)


def spread_weights(query_weight, key_weight, value_weight, sides):
    own = jnp.concatenate([query_weight, key_weight, value_weight], axis=1)
    other = cycled(own, "far", 1)
    own, other, _ = lax.optimization_barrier((own, other, sides))
    far = lax.axis_index("far")
    both = jnp.where(far == 0, jnp.stack([own, other]), jnp.stack([other, own]))
    return lax.all_gather(both, ("z", "core"), axis=0, tiled=False)


def shards(features, query_weight, key_weight, value_weight, doc_lengths, out_grad):
    tok_rows, slab_rows = features.shape
    query_cols = query_weight.shape[1]
    value_cols = key_weight.shape[1]
    query_scale = (slab_rows * 16 / HEADS_Q) ** (-0.5)
    ctx_index = lax.axis_index(CTX)

    arrays, pieces, sides = spread_features(features.T.reshape(2, slab_rows // 2, tok_rows))
    weights = spread_weights(query_weight, key_weight, value_weight, sides)
    step = jnp.arange(4, dtype=jnp.int32)
    x_at, y_at = lax.axis_index("x"), lax.axis_index("y")
    place = ((x_at + step) % 4)[:, None] * 4 + ((y_at + step) % 4)[None, :]
    place = jnp.concatenate([place.reshape(16), jnp.stack([lax.axis_index("core"), y_at])])
    place = place.astype(jnp.int32)

    starts = jnp.cumsum(doc_lengths) - doc_lengths
    query_index = ctx_index * tok_rows + jnp.arange(tok_rows, dtype=jnp.int32)
    query_start = start_of(query_index, starts)
    tables = rope_tables(query_index - query_start)
    low = jnp.maximum(query_start, query_index - (WINDOW - 1)) - (ctx_index - SPAN) * tok_rows
    low = low.astype(jnp.int32)[None]

    key_value = project(
        key_value_kernel,
        jax.ShapeDtypeStruct((2, tok_rows, HEAD_DIM), jnp.bfloat16),
        arrays,
        pieces,
        (query_cols, query_cols + 2 * value_cols),
        place,
        weights,
        tables,
    )
    far, near = passed_along(key_value, 2), passed_along(key_value, 1)
    queries = project(
        functools.partial(query_kernel, scale=query_scale),
        jax.ShapeDtypeStruct((tok_rows, query_cols), jnp.bfloat16),
        arrays,
        pieces,
        (0, query_cols),
        place,
        weights,
        tables,
    )
    attention, far_part, near_part, own_part = attention_call(
        low, queries, far, near, key_value, out_grad
    )
    far_back, near_back = passed_along(far_part, -2), passed_along(near_part, -1)
    kept, sent = weight_grad(arrays, pieces, place, own_part, near_back, far_back, tables)
    weight_grads = scattered_sum(kept, sent).astype(jnp.bfloat16)
    return attention, weight_grads[:, :value_cols], weight_grads[:, value_cols:]


def solution(mesh):
    sizes = (mesh.shape["ctx"] // 4, 2, 2, 4, 4)
    torus = Mesh(mesh.devices.reshape(sizes), CTX + HEAD)
    placed = (P(CTX, HEAD), P(CTX, HEAD), P(CTX, HEAD), P(CTX, HEAD), P(), P(CTX, HEAD))
    return jax.shard_map(
        shards,
        mesh=torus,
        in_specs=placed,
        out_specs=(P(CTX, HEAD), P(CTX, HEAD), P(CTX, HEAD)),
        check_vma=False,
    )
```

```python
import functools

import jax
import jax.numpy as jnp
from jax import lax
from jax.experimental import pallas as pl
from jax.experimental.pallas import tpu as pltpu
from jax.sharding import Mesh
from jax.sharding import PartitionSpec as P


HEADS_Q = 32
HEAD_DIM = 128
WINDOW = 1024
SPAN = 2
CORES = 2
CTX = ("z", "far", "core")
HEAD = ("x", "y")
ROPE_BASE = 10000.0


def cycled(value, axis, step):
    count = lax.axis_size(axis)
    return lax.ppermute(value, axis, [(i, (i + step) % count) for i in range(count)])


def passed_along(block, distance):
    devices = range(lax.axis_size(CTX))
    route = [(i - distance, i) for i in devices if i - distance in devices]
    return lax.ppermute(block, CTX, route)


def rope_tables(offsets):
    middle = HEAD_DIM // 2
    inverse = ROPE_BASE ** (-(jnp.arange(middle).astype(jnp.float32) * 2.0 / HEAD_DIM))
    angles = offsets.astype(jnp.float32)[:, None] * inverse[None, :]
    cosine = jnp.cos(angles)
    sine = jnp.sin(angles)
    return (
        jnp.concatenate([cosine, cosine], axis=-1),
        jnp.concatenate([-sine, sine], axis=-1),
    )


def start_of(positions, starts):
    candidates = jnp.where(starts[None, :] <= positions[:, None], starts[None, :], -1)
    return jnp.max(candidates, axis=1)


def spread_features(own):
    arrays, pieces = [], []

    def add(array, entries):
        for at, (x_step, y_step, half) in enumerate(entries):
            pieces.append((len(arrays), at, x_step, y_step, half))
        arrays.append(array)

    def across(batch, y_steps, x_steps):
        halves = [(y_step, half) for y_step in y_steps for half in range(2)]
        add(batch, [(0, *entry) for entry in halves])
        for x_step in x_steps:
            moved = cycled(batch, "x", -x_step)
            add(moved, [(x_step, *entry) for entry in halves])

    row = lax.all_gather(own, "x", axis=0, tiled=True)
    add(row, [(-1 - x_at, 0, half) for x_at in range(4) for half in range(2)])
    above = cycled(own, "y", 1)
    below = cycled(own, "y", -1)
    sides = jnp.concatenate([above, below])
    across(sides, (3, 1), (1, 3))
    own, sides = lax.optimization_barrier((own, sides))
    opposite = cycled(own, "y", 2)
    x_at = lax.axis_index("x")
    facing = lax.dynamic_slice_in_dim(row, 2 * ((x_at + 2) % 4), 2, 0)
    for y_step in (3, 1):
        moved = cycled(facing, "y", -y_step)
        add(moved, [(2, y_step, 0), (2, y_step, 1)])
    across(opposite, (2,), (1, 3, 2))
    return arrays, pieces, sides


def place_of(place_ref, x_step, y_step):
    if x_step < 0:
        return (-1 - x_step) * 4 + place_ref[17]
    return place_ref[x_step * 4 + y_step]


CONTRACT_ROWS = (((0,), (0,)), ((), ()))
CONTRACT_COLS = (((1,), (1,)), ((), ()))
BLOCK = 256


def turned(values, cosine, sine_signed):
    return values * cosine + pltpu.roll(values, HEAD_DIM // 2, 1) * sine_signed


def unturned(values, cosine, sine_signed):
    return values * cosine - pltpu.roll(values, HEAD_DIM // 2, 1) * sine_signed


def accumulated(pieces, columns, place_ref, weights_ref, arrays, total, buffer, arrived, *held):
    first, last = columns

    def fetch_weight(number):
        _, _, x_step, y_step, half = pieces[number]
        place = place_of(place_ref, x_step, y_step)
        return pltpu.make_async_copy(
            weights_ref.at[(place // 2) * CORES + half, place % 2, :, first:last],
            buffer.at[number],
            arrived.at[number],
        )

    def fetch_array(array):
        return pltpu.make_async_copy(arrays[array], held[array], arrived.at[len(pieces) + array])

    for number, (array, at, *_) in enumerate(pieces):
        if at == 0:
            fetch_array(array).start()
        fetch_weight(number).start()
    for number, (array, at, *_) in enumerate(pieces):
        if at == 0:
            fetch_array(array).wait()
        fetch_weight(number).wait()
        term = lax.dot_general(
            held[array][at], buffer[number], CONTRACT_ROWS, preferred_element_type=jnp.float32
        )
        total[...] = term if number == 0 else total[...] + term


def key_value_kernel(pieces, columns, place_ref, weights_ref, cos_ref, sin_ref, *refs):
    count = 1 + pieces[-1][0]
    arrays, (out_ref, total, *work) = refs[:count], refs[count:]
    accumulated(pieces, columns, place_ref, weights_ref, arrays, total, *work)
    keys = turned(total[:, :HEAD_DIM], cos_ref[...], sin_ref[...])
    out_ref[0] = keys.astype(jnp.bfloat16)
    out_ref[1] = total[:, HEAD_DIM:].astype(jnp.bfloat16)


def query_kernel(pieces, columns, place_ref, weights_ref, cos_ref, sin_ref, *refs, scale):
    count = 1 + pieces[-1][0]
    arrays, (out_ref, total, *work) = refs[:count], refs[count:]
    accumulated(pieces, columns, place_ref, weights_ref, arrays, total, *work)
    for head in range((columns[1] - columns[0]) // HEAD_DIM):
        part = total[:, head * HEAD_DIM : (head + 1) * HEAD_DIM]
        queries = turned(part, cos_ref[...], sin_ref[...]) * scale
        out_ref[:, head * HEAD_DIM : (head + 1) * HEAD_DIM] = queries.astype(jnp.bfloat16)


def attention_kernel(low_ref, q_ref, far_ref, near_ref, own_ref, grad_ref, att_ref, *refs):
    far_out, near_out, own_out, keys, values, acc = refs
    tokens, width = q_ref.shape
    for number, ref in enumerate((far_ref, near_ref, own_ref)):
        keys[number * tokens : (number + 1) * tokens] = ref[0]
        values[number * tokens : (number + 1) * tokens] = ref[1]
    acc[...] = jnp.zeros_like(acc)
    span = 2 * tokens + BLOCK
    heads = width // HEAD_DIM
    for head in range(heads):
        cols = slice(head * HEAD_DIM, (head + 1) * HEAD_DIM)
        for at in range(0, tokens, BLOCK):
            rows = slice(at, at + BLOCK)
            window = slice(at, at + span)
            low = low_ref[:, rows]
            key_at = lax.broadcasted_iota(jnp.int32, (span, BLOCK), 0) + at
            query_at = lax.broadcasted_iota(jnp.int32, (span, BLOCK), 1) + (2 * tokens + at)
            allowed = (key_at >= low) & (key_at <= query_at)
            query = q_ref[rows, cols]
            grad = grad_ref[rows, cols]
            scores = lax.dot_general(
                keys[window], query, CONTRACT_COLS, preferred_element_type=jnp.float32
            )
            scores = jnp.where(allowed, scores, -jnp.inf)
            raw = jnp.exp(scores - jnp.max(scores, axis=0, keepdims=True))
            probs = raw * (1.0 / jnp.sum(raw, axis=0, keepdims=True))
            low_probs = probs.astype(jnp.bfloat16)
            attended = lax.dot_general(
                values[window], low_probs, CONTRACT_ROWS, preferred_element_type=jnp.float32
            )
            attended = attended.T.astype(jnp.bfloat16)
            att_ref[rows, cols] = attended
            product = grad.astype(jnp.float32) * attended.astype(jnp.float32)
            out_dot = jnp.sum(product.T, axis=0, keepdims=True)
            acc[1, window] += jnp.dot(low_probs, grad, preferred_element_type=jnp.float32)
            prob_grad = lax.dot_general(
                values[window], grad, CONTRACT_COLS, preferred_element_type=jnp.float32
            )
            score_grad = (probs * (prob_grad - out_dot)).astype(jnp.bfloat16)
            acc[0, window] += jnp.dot(score_grad, query, preferred_element_type=jnp.float32)
    far_out[...] = acc[:, :tokens].astype(jnp.bfloat16)
    near_out[...] = acc[:, tokens : 2 * tokens].astype(jnp.bfloat16)
    own_out[...] = acc[:, 2 * tokens :]


def attention_call(low, queries, far, near, own, grads):
    tokens, width = queries.shape
    vmem = pl.BlockSpec(memory_space=pltpu.VMEM)
    block = jax.ShapeDtypeStruct(own.shape, jnp.bfloat16)
    pairs = tokens * (2 * tokens + BLOCK) * (width // HEAD_DIM)
    return pl.pallas_call(
        attention_kernel,
        out_shape=(
            jax.ShapeDtypeStruct((tokens, width), jnp.bfloat16),
            block,
            block,
            jax.ShapeDtypeStruct(own.shape, jnp.float32),
        ),
        in_specs=[vmem] * 6,
        out_specs=(vmem,) * 4,
        scratch_shapes=[
            pltpu.VMEM((3 * tokens, HEAD_DIM), jnp.bfloat16),
            pltpu.VMEM((3 * tokens, HEAD_DIM), jnp.bfloat16),
            pltpu.VMEM((2, 3 * tokens, HEAD_DIM), jnp.float32),
        ],
        compiler_params=pltpu.CompilerParams(vmem_limit_bytes=20 << 20),
        cost_estimate=pl.CostEstimate(
            flops=10 * pairs * HEAD_DIM,
            bytes_accessed=4 * tokens * width * 4,
            transcendentals=pairs,
        ),
        name="attention",
    )(low, queries, far, near, own, grads)


def project(kernel, out_shape, arrays, pieces, columns, place, weights, tables):
    tokens = arrays[0].shape[2]
    width = columns[1] - columns[0]
    depth = len(pieces) * arrays[0].shape[1]
    vmem, hbm = (pl.BlockSpec(memory_space=space) for space in (pltpu.VMEM, pltpu.HBM))
    return pl.pallas_call(
        functools.partial(kernel, pieces, columns),
        out_shape=out_shape,
        in_specs=[pl.BlockSpec(memory_space=pltpu.SMEM), hbm, vmem, vmem] + [hbm] * len(arrays),
        out_specs=vmem,
        scratch_shapes=[
            pltpu.VMEM((tokens, width), jnp.float32),
            pltpu.VMEM((len(pieces), arrays[0].shape[1], width), jnp.bfloat16),
            pltpu.SemaphoreType.DMA((len(pieces) + len(arrays),)),
        ]
        + [pltpu.VMEM(array.shape, array.dtype) for array in arrays],
        compiler_params=pltpu.CompilerParams(vmem_limit_bytes=60 << 20),
        cost_estimate=pl.CostEstimate(
            flops=2 * tokens * depth * width,
            bytes_accessed=2 * depth * (tokens + width) + 4 * tokens * width,
            transcendentals=0,
        ),
        name="project",
    )(place, weights, *tables, *arrays)


def weight_grad_kernel(
    pieces, partner, place_ref, own_ref, near_ref, far_ref, cos_ref, sin_ref, *refs
):
    count = 1 + pieces[-1][0]
    arrays, (out_ref, held, arrived) = refs[:count], refs[count:]
    core = place_ref[16]
    wanted = 1 - core if partner else core
    slabs = [piece for piece in pieces if piece[4] == 0]

    def fetch(number):
        array, at, *_ = slabs[number]
        return pltpu.make_async_copy(
            arrays[array].at[at + wanted], held.at[number], arrived.at[number]
        )

    for number in range(len(slabs)):
        fetch(number).start()
    sums = [
        own_ref[i] + near_ref[i].astype(jnp.float32) + far_ref[i].astype(jnp.float32)
        for i in range(2)
    ]
    key_grad = unturned(sums[0], cos_ref[...], sin_ref[...])
    grads = jnp.concatenate([key_grad, sums[1]], axis=1).astype(jnp.bfloat16)
    for number, (_, _, x_step, y_step, _) in enumerate(slabs):
        fetch(number).wait()
        term = jnp.dot(held[number], grads, preferred_element_type=jnp.float32)
        out_ref[place_of(place_ref, x_step, y_step)] = term.astype(jnp.bfloat16)


def weight_grad(arrays, pieces, place, own, near, far, tables, partner):
    rows, tokens = arrays[0].shape[1:]
    width = 2 * HEAD_DIM
    vmem, hbm = (pl.BlockSpec(memory_space=space) for space in (pltpu.VMEM, pltpu.HBM))
    depth = len(pieces) * rows // 2
    return pl.pallas_call(
        functools.partial(weight_grad_kernel, pieces, partner),
        out_shape=jax.ShapeDtypeStruct((16, rows, width), jnp.bfloat16),
        in_specs=[pl.BlockSpec(memory_space=pltpu.SMEM)] + [vmem] * 5 + [hbm] * len(arrays),
        out_specs=vmem,
        scratch_shapes=[
            pltpu.VMEM((16, rows, tokens), jnp.bfloat16),
            pltpu.SemaphoreType.DMA((16,)),
        ],
        compiler_params=pltpu.CompilerParams(vmem_limit_bytes=60 << 20),
        cost_estimate=pl.CostEstimate(
            flops=2 * tokens * depth * width,
            bytes_accessed=2 * depth * (tokens + width) + 2 * tokens * width,
            transcendentals=0,
        ),
        name="weight_grad",
    )(place, own, near, far, *tables, *arrays)


def scattered_sum(kept, sent):
    chip = kept.astype(jnp.float32) + cycled(sent, "core", 1).astype(jnp.float32)
    chip = chip.astype(jnp.bfloat16)
    landed = lax.all_to_all(chip, ("z", "far"), 0, 0, tiled=True)
    return jnp.sum(landed.astype(jnp.float32), axis=0)


def spread_weights(query_weight, key_weight, value_weight, sides):
    own = jnp.concatenate([query_weight, key_weight, value_weight], axis=1)
    other = cycled(own, "far", 1)
    own, other, _ = lax.optimization_barrier((own, other, sides))
    far = lax.axis_index("far")
    both = jnp.where(far == 0, jnp.stack([own, other]), jnp.stack([other, own]))
    return lax.all_gather(both, ("z", "core"), axis=0, tiled=False)


def shards(features, query_weight, key_weight, value_weight, doc_lengths, out_grad):
    tok_rows, slab_rows = features.shape
    query_cols = query_weight.shape[1]
    value_cols = key_weight.shape[1]
    query_scale = (slab_rows * 16 / HEADS_Q) ** (-0.5)
    ctx_index = lax.axis_index(CTX)

    arrays, pieces, sides = spread_features(features.T.reshape(2, slab_rows // 2, tok_rows))
    weights = spread_weights(query_weight, key_weight, value_weight, sides)
    step = jnp.arange(4, dtype=jnp.int32)
    x_at, y_at = lax.axis_index("x"), lax.axis_index("y")
    place = ((x_at + step) % 4)[:, None] * 4 + ((y_at + step) % 4)[None, :]
    place = jnp.concatenate([place.reshape(16), jnp.stack([lax.axis_index("core"), y_at])])
    place = place.astype(jnp.int32)

    starts = jnp.cumsum(doc_lengths) - doc_lengths
    query_index = ctx_index * tok_rows + jnp.arange(tok_rows, dtype=jnp.int32)
    query_start = start_of(query_index, starts)
    tables = rope_tables(query_index - query_start)
    low = jnp.maximum(query_start, query_index - (WINDOW - 1)) - (ctx_index - SPAN) * tok_rows
    low = low.astype(jnp.int32)[None]

    key_value = project(
        key_value_kernel,
        jax.ShapeDtypeStruct((2, tok_rows, HEAD_DIM), jnp.bfloat16),
        arrays,
        pieces,
        (query_cols, query_cols + 2 * value_cols),
        place,
        weights,
        tables,
    )
    far, near = passed_along(key_value, 2), passed_along(key_value, 1)
    queries = project(
        functools.partial(query_kernel, scale=query_scale),
        jax.ShapeDtypeStruct((tok_rows, query_cols), jnp.bfloat16),
        arrays,
        pieces,
        (0, query_cols),
        place,
        weights,
        tables,
    )
    attention, far_part, near_part, own_part = attention_call(
        low, queries, far, near, key_value, out_grad
    )
    far_back, near_back = passed_along(far_part, -2), passed_along(near_part, -1)
    sent, kept = (
        weight_grad(arrays, pieces, place, own_part, near_back, far_back, tables, partner)
        for partner in (True, False)
    )
    weight_grads = scattered_sum(kept, sent).astype(jnp.bfloat16)
    return attention, weight_grads[:, :value_cols], weight_grads[:, value_cols:]


def solution(mesh):
    sizes = (mesh.shape["ctx"] // 4, 2, 2, 4, 4)
    torus = Mesh(mesh.devices.reshape(sizes), CTX + HEAD)
    placed = (P(CTX, HEAD), P(CTX, HEAD), P(CTX, HEAD), P(CTX, HEAD), P(), P(CTX, HEAD))
    return jax.shard_map(
        shards,
        mesh=torus,
        in_specs=placed,
        out_specs=(P(CTX, HEAD), P(CTX, HEAD), P(CTX, HEAD)),
        check_vma=False,
    )
```

```python
import functools

import jax
import jax.numpy as jnp
from jax import lax
from jax.experimental import pallas as pl
from jax.experimental.pallas import tpu as pltpu
from jax.sharding import Mesh
from jax.sharding import PartitionSpec as P


HEADS_Q = 32
HEAD_DIM = 128
WINDOW = 1024
SPAN = 2
CORES = 2
CTX = ("z", "far", "core")
HEAD = ("x", "y")
ROPE_BASE = 10000.0


def cycled(value, axis, step):
    count = lax.axis_size(axis)
    return lax.ppermute(value, axis, [(i, (i + step) % count) for i in range(count)])


def passed_along(block, distance):
    devices = range(lax.axis_size(CTX))
    route = [(i - distance, i) for i in devices if i - distance in devices]
    return lax.ppermute(block, CTX, route)


def rope_tables(offsets):
    middle = HEAD_DIM // 2
    inverse = ROPE_BASE ** (-(jnp.arange(middle).astype(jnp.float32) * 2.0 / HEAD_DIM))
    angles = offsets.astype(jnp.float32)[:, None] * inverse[None, :]
    cosine = jnp.cos(angles)
    sine = jnp.sin(angles)
    return (
        jnp.concatenate([cosine, cosine], axis=-1),
        jnp.concatenate([-sine, sine], axis=-1),
    )


def start_of(positions, starts):
    candidates = jnp.where(starts[None, :] <= positions[:, None], starts[None, :], -1)
    return jnp.max(candidates, axis=1)


def spread_features(own):
    arrays, pieces = [], []

    def add(array, entries):
        for at, (x_step, y_step, half) in enumerate(entries):
            pieces.append((len(arrays), at, x_step, y_step, half))
        arrays.append(array)

    def across(batch, y_steps, x_steps):
        halves = [(y_step, half) for y_step in y_steps for half in range(2)]
        add(batch, [(0, *entry) for entry in halves])
        for x_step in x_steps:
            moved = cycled(batch, "x", -x_step)
            add(moved, [(x_step, *entry) for entry in halves])

    above = cycled(own, "y", 1)
    below = cycled(own, "y", -1)
    across(own, (0,), (1, 3, 2))
    sides = jnp.concatenate([above, below])
    across(sides, (3, 1), (1, 3, 2))
    own, sides = lax.optimization_barrier((own, sides))
    opposite = cycled(own, "y", 2)
    across(opposite, (2,), (1, 3, 2))
    return arrays, pieces, sides


CONTRACT_ROWS = (((0,), (0,)), ((), ()))
CONTRACT_COLS = (((1,), (1,)), ((), ()))
BLOCK = 256


def turned(values, cosine, sine_signed):
    return values * cosine + pltpu.roll(values, HEAD_DIM // 2, 1) * sine_signed


def unturned(values, cosine, sine_signed):
    return values * cosine - pltpu.roll(values, HEAD_DIM // 2, 1) * sine_signed


def accumulated(pieces, columns, place_ref, weights_ref, arrays, total):
    first, last = columns
    for number, (array, at, x_step, y_step, half) in enumerate(pieces):
        place = place_ref[x_step * 4 + y_step]
        weight = weights_ref[(place // 2) * CORES + half, place % 2, :, first:last]
        term = lax.dot_general(
            arrays[array][at], weight, CONTRACT_ROWS, preferred_element_type=jnp.float32
        )
        total[...] = term if number == 0 else total[...] + term


def key_value_kernel(pieces, columns, place_ref, weights_ref, cos_ref, sin_ref, *refs):
    *arrays, out_ref, total = refs
    accumulated(pieces, columns, place_ref, weights_ref, arrays, total)
    keys = turned(total[:, :HEAD_DIM], cos_ref[...], sin_ref[...])
    out_ref[0] = keys.astype(jnp.bfloat16)
    out_ref[1] = total[:, HEAD_DIM:].astype(jnp.bfloat16)


def query_kernel(pieces, columns, place_ref, weights_ref, cos_ref, sin_ref, *refs, scale):
    *arrays, out_ref, total = refs
    accumulated(pieces, columns, place_ref, weights_ref, arrays, total)
    for head in range((columns[1] - columns[0]) // HEAD_DIM):
        part = total[:, head * HEAD_DIM : (head + 1) * HEAD_DIM]
        queries = turned(part, cos_ref[...], sin_ref[...]) * scale
        out_ref[:, head * HEAD_DIM : (head + 1) * HEAD_DIM] = queries.astype(jnp.bfloat16)


def attention_kernel(low_ref, q_ref, far_ref, near_ref, own_ref, grad_ref, att_ref, *refs):
    far_out, near_out, own_out, keys, values, acc = refs
    tokens, width = q_ref.shape
    for number, ref in enumerate((far_ref, near_ref, own_ref)):
        keys[number * tokens : (number + 1) * tokens] = ref[0]
        values[number * tokens : (number + 1) * tokens] = ref[1]
    acc[...] = jnp.zeros_like(acc)
    span = 2 * tokens + BLOCK
    heads = width // HEAD_DIM
    for head in range(heads):
        cols = slice(head * HEAD_DIM, (head + 1) * HEAD_DIM)
        for at in range(0, tokens, BLOCK):
            rows = slice(at, at + BLOCK)
            window = slice(at, at + span)
            low = low_ref[:, rows]
            key_at = lax.broadcasted_iota(jnp.int32, (span, BLOCK), 0) + at
            query_at = lax.broadcasted_iota(jnp.int32, (span, BLOCK), 1) + (2 * tokens + at)
            allowed = (key_at >= low) & (key_at <= query_at)
            query = q_ref[rows, cols]
            grad = grad_ref[rows, cols]
            scores = lax.dot_general(
                keys[window], query, CONTRACT_COLS, preferred_element_type=jnp.float32
            )
            scores = jnp.where(allowed, scores, -jnp.inf)
            raw = jnp.exp(scores - jnp.max(scores, axis=0, keepdims=True))
            probs = raw * (1.0 / jnp.sum(raw, axis=0, keepdims=True))
            low_probs = probs.astype(jnp.bfloat16)
            attended = lax.dot_general(
                values[window], low_probs, CONTRACT_ROWS, preferred_element_type=jnp.float32
            )
            attended = attended.T.astype(jnp.bfloat16)
            att_ref[rows, cols] = attended
            product = grad.astype(jnp.float32) * attended.astype(jnp.float32)
            out_dot = jnp.sum(product.T, axis=0, keepdims=True)
            acc[1, window] += jnp.dot(low_probs, grad, preferred_element_type=jnp.float32)
            prob_grad = lax.dot_general(
                values[window], grad, CONTRACT_COLS, preferred_element_type=jnp.float32
            )
            score_grad = (probs * (prob_grad - out_dot)).astype(jnp.bfloat16)
            acc[0, window] += jnp.dot(score_grad, query, preferred_element_type=jnp.float32)
    far_out[...] = acc[:, :tokens].astype(jnp.bfloat16)
    near_out[...] = acc[:, tokens : 2 * tokens].astype(jnp.bfloat16)
    own_out[...] = acc[:, 2 * tokens :]


def attention_call(low, queries, far, near, own, grads):
    tokens, width = queries.shape
    vmem = pl.BlockSpec(memory_space=pltpu.VMEM)
    block = jax.ShapeDtypeStruct(own.shape, jnp.bfloat16)
    pairs = tokens * (2 * tokens + BLOCK) * (width // HEAD_DIM)
    return pl.pallas_call(
        attention_kernel,
        out_shape=(
            jax.ShapeDtypeStruct((tokens, width), jnp.bfloat16),
            block,
            block,
            jax.ShapeDtypeStruct(own.shape, jnp.float32),
        ),
        in_specs=[vmem] * 6,
        out_specs=(vmem,) * 4,
        scratch_shapes=[
            pltpu.VMEM((3 * tokens, HEAD_DIM), jnp.bfloat16),
            pltpu.VMEM((3 * tokens, HEAD_DIM), jnp.bfloat16),
            pltpu.VMEM((2, 3 * tokens, HEAD_DIM), jnp.float32),
        ],
        compiler_params=pltpu.CompilerParams(vmem_limit_bytes=10 << 20),
        cost_estimate=pl.CostEstimate(
            flops=10 * pairs * HEAD_DIM,
            bytes_accessed=4 * tokens * width * 4,
            transcendentals=pairs,
        ),
        name="attention",
    )(low, queries, far, near, own, grads)


def project(kernel, out_shape, arrays, pieces, columns, place, weights, tables):
    tokens = arrays[0].shape[2]
    width = columns[1] - columns[0]
    depth = len(pieces) * arrays[0].shape[1]
    vmem = pl.BlockSpec(memory_space=pltpu.VMEM)
    return pl.pallas_call(
        functools.partial(kernel, pieces, columns),
        out_shape=out_shape,
        in_specs=[pl.BlockSpec(memory_space=pltpu.SMEM)] + [vmem] * (3 + len(arrays)),
        out_specs=vmem,
        scratch_shapes=[pltpu.VMEM((tokens, width), jnp.float32)],
        compiler_params=pltpu.CompilerParams(vmem_limit_bytes=10 << 20),
        cost_estimate=pl.CostEstimate(
            flops=2 * tokens * depth * width,
            bytes_accessed=2 * depth * (tokens + width) + 4 * tokens * width,
            transcendentals=0,
        ),
        name="project",
    )(place, weights, *tables, *arrays)


def weight_grad_kernel(
    pieces, partner, place_ref, own_ref, near_ref, far_ref, cos_ref, sin_ref, *refs
):
    *arrays, out_ref, grads = refs
    core = place_ref[16]
    wanted = 1 - core if partner else core
    sums = [
        own_ref[i] + near_ref[i].astype(jnp.float32) + far_ref[i].astype(jnp.float32)
        for i in range(2)
    ]
    grads[:, :HEAD_DIM] = unturned(sums[0], cos_ref[...], sin_ref[...]).astype(jnp.bfloat16)
    grads[:, HEAD_DIM:] = sums[1].astype(jnp.bfloat16)
    for array, at, x_step, y_step, half in pieces:
        if half == 0:
            term = jnp.dot(
                arrays[array][at + wanted], grads[...], preferred_element_type=jnp.float32
            )
            out_ref[place_ref[x_step * 4 + y_step]] = term.astype(jnp.bfloat16)


def weight_grad(arrays, pieces, place, own, near, far, tables, partner):
    rows, tokens = arrays[0].shape[1:]
    width = 2 * HEAD_DIM
    vmem = pl.BlockSpec(memory_space=pltpu.VMEM)
    depth = len(pieces) * rows // 2
    return pl.pallas_call(
        functools.partial(weight_grad_kernel, pieces, partner),
        out_shape=jax.ShapeDtypeStruct((16, rows, width), jnp.bfloat16),
        in_specs=[pl.BlockSpec(memory_space=pltpu.SMEM)] + [vmem] * (5 + len(arrays)),
        out_specs=vmem,
        scratch_shapes=[pltpu.VMEM((tokens, width), jnp.bfloat16)],
        compiler_params=pltpu.CompilerParams(vmem_limit_bytes=10 << 20),
        cost_estimate=pl.CostEstimate(
            flops=2 * tokens * depth * width,
            bytes_accessed=2 * depth * (tokens + width) + 2 * tokens * width,
            transcendentals=0,
        ),
        name="weight_grad",
    )(place, own, near, far, *tables, *arrays)


def scattered_sum(kept, sent):
    chip = kept.astype(jnp.float32) + cycled(sent, "core", 1).astype(jnp.float32)
    chip = chip.astype(jnp.bfloat16)
    landed = lax.all_to_all(chip, ("z", "far"), 0, 0, tiled=True)
    return jnp.sum(landed.astype(jnp.float32), axis=0)


def spread_weights(query_weight, key_weight, value_weight):
    own = jnp.concatenate([query_weight, key_weight, value_weight], axis=1)
    other = cycled(own, "far", 1)
    far = lax.axis_index("far")
    both = jnp.where(far == 0, jnp.stack([own, other]), jnp.stack([other, own]))
    return lax.all_gather(both, ("z", "core"), axis=0, tiled=False)


def shards(features, query_weight, key_weight, value_weight, doc_lengths, out_grad):
    tok_rows, slab_rows = features.shape
    query_cols = query_weight.shape[1]
    value_cols = key_weight.shape[1]
    query_scale = (slab_rows * 16 / HEADS_Q) ** (-0.5)
    ctx_index = lax.axis_index(CTX)

    arrays, pieces, _ = spread_features(features.T.reshape(2, slab_rows // 2, tok_rows))
    weights = spread_weights(query_weight, key_weight, value_weight)
    step = jnp.arange(4, dtype=jnp.int32)
    x_at, y_at = lax.axis_index("x"), lax.axis_index("y")
    place = ((x_at + step) % 4)[:, None] * 4 + ((y_at + step) % 4)[None, :]
    place = jnp.concatenate([place.reshape(16), jnp.stack([lax.axis_index("core"), y_at])])
    place = place.astype(jnp.int32)

    starts = jnp.cumsum(doc_lengths) - doc_lengths
    query_index = ctx_index * tok_rows + jnp.arange(tok_rows, dtype=jnp.int32)
    query_start = start_of(query_index, starts)
    tables = rope_tables(query_index - query_start)
    low = jnp.maximum(query_start, query_index - (WINDOW - 1)) - (ctx_index - SPAN) * tok_rows
    low = low.astype(jnp.int32)[None]

    key_value = project(
        key_value_kernel,
        jax.ShapeDtypeStruct((2, tok_rows, HEAD_DIM), jnp.bfloat16),
        arrays,
        pieces,
        (query_cols, query_cols + 2 * value_cols),
        place,
        weights,
        tables,
    )
    far, near = passed_along(key_value, 2), passed_along(key_value, 1)
    queries = project(
        functools.partial(query_kernel, scale=query_scale),
        jax.ShapeDtypeStruct((tok_rows, query_cols), jnp.bfloat16),
        arrays,
        pieces,
        (0, query_cols),
        place,
        weights,
        tables,
    )
    attention, far_part, near_part, own_part = attention_call(
        low, queries, far, near, key_value, out_grad
    )
    far_back, near_back = passed_along(far_part, -2), passed_along(near_part, -1)
    sent, kept = (
        weight_grad(arrays, pieces, place, own_part, near_back, far_back, tables, partner)
        for partner in (True, False)
    )
    weight_grads = scattered_sum(kept, sent).astype(jnp.bfloat16)
    return attention, weight_grads[:, :value_cols], weight_grads[:, value_cols:]


def solution(mesh):
    sizes = (mesh.shape["ctx"] // 4, 2, 2, 4, 4)
    torus = Mesh(mesh.devices.reshape(sizes), CTX + HEAD)
    placed = (P(CTX, HEAD), P(CTX, HEAD), P(CTX, HEAD), P(CTX, HEAD), P(), P(CTX, HEAD))
    return jax.shard_map(
        shards,
        mesh=torus,
        in_specs=placed,
        out_specs=(P(CTX, HEAD), P(CTX, HEAD), P(CTX, HEAD)),
        check_vma=False,
    )
```

```python
import functools

import jax
import jax.numpy as jnp
from jax import lax
from jax.experimental import pallas as pl
from jax.experimental.pallas import tpu as pltpu
from jax.sharding import Mesh
from jax.sharding import PartitionSpec as P


HEADS_Q = 32
HEAD_DIM = 128
WINDOW = 1024
SPAN = 2
CORES = 2
CTX = ("z", "far", "core")
HEAD = ("x", "y")
ROPE_BASE = 10000.0


def cycled(value, axis, step):
    count = lax.axis_size(axis)
    return lax.ppermute(value, axis, [(i, (i + step) % count) for i in range(count)])


def passed_along(block, distance):
    devices = range(lax.axis_size(CTX))
    route = [(i - distance, i) for i in devices if i - distance in devices]
    return lax.ppermute(block, CTX, route)


def rope_tables(offsets):
    middle = HEAD_DIM // 2
    inverse = ROPE_BASE ** (-(jnp.arange(middle).astype(jnp.float32) * 2.0 / HEAD_DIM))
    angles = offsets.astype(jnp.float32)[:, None] * inverse[None, :]
    cosine = jnp.cos(angles)
    sine = jnp.sin(angles)
    return (
        jnp.concatenate([cosine, cosine], axis=-1),
        jnp.concatenate([-sine, sine], axis=-1),
    )


def start_of(positions, starts):
    candidates = jnp.where(starts[None, :] <= positions[:, None], starts[None, :], -1)
    return jnp.max(candidates, axis=1)


def spread_features(own):
    arrays, pieces = [], []

    def add(array, entries):
        for at, (x_step, y_step, half) in enumerate(entries):
            pieces.append((len(arrays), at, x_step, y_step, half))
        arrays.append(array)

    def across(batch, y_steps, x_steps):
        halves = [(y_step, half) for y_step in y_steps for half in range(2)]
        add(batch, [(0, *entry) for entry in halves])
        for x_step in x_steps:
            moved = cycled(batch, "x", -x_step)
            add(moved, [(x_step, *entry) for entry in halves])

    above = cycled(own, "y", 1)
    below = cycled(own, "y", -1)
    across(own, (0,), (1, 3, 2))
    sides = jnp.concatenate([above, below])
    across(sides, (3, 1), (1, 3))
    early = len(arrays)
    opposite = cycled(own, "y", 2)
    across(opposite, (2,), (1, 3, 2))
    right, left = arrays[early - 2 : early]
    for moved, x_shift, y_step in ((left[:2], 1, 3), (right[2:], -1, 1)):
        moved = cycled(moved, "x", x_shift)
        add(moved, [(2, y_step, 0), (2, y_step, 1)])
    return arrays, pieces, early


CONTRACT_ROWS = (((0,), (0,)), ((), ()))
CONTRACT_COLS = (((1,), (1,)), ((), ()))
BLOCK = 256


def turned(values, cosine, sine_signed):
    return values * cosine + pltpu.roll(values, HEAD_DIM // 2, 1) * sine_signed


def unturned(values, cosine, sine_signed):
    return values * cosine - pltpu.roll(values, HEAD_DIM // 2, 1) * sine_signed


def accumulated(pieces, columns, place_ref, weights_ref, arrays, total, begun=None):
    first, last = columns
    for number, (array, at, x_step, y_step, half) in enumerate(pieces):
        place = place_ref[x_step * 4 + y_step]
        weight = weights_ref[(place // 2) * CORES + half, place % 2, :, first:last]
        term = lax.dot_general(
            arrays[array][at], weight, CONTRACT_ROWS, preferred_element_type=jnp.float32
        )
        if number == 0:
            total[...] = term if begun is None else begun[...] + term
        else:
            total[...] += term


def partial_kernel(pieces, columns, place_ref, weights_ref, cos_ref, sin_ref, *refs):
    *arrays, out_ref, total = refs
    accumulated(pieces, columns, place_ref, weights_ref, arrays, total)
    out_ref[...] = total[...]


def key_value_kernel(pieces, columns, place_ref, weights_ref, cos_ref, sin_ref, *refs):
    *arrays, begun, out_ref, total = refs
    accumulated(pieces, columns, place_ref, weights_ref, arrays, total, begun)
    keys = turned(total[:, :HEAD_DIM], cos_ref[...], sin_ref[...])
    out_ref[0] = keys.astype(jnp.bfloat16)
    out_ref[1] = total[:, HEAD_DIM:].astype(jnp.bfloat16)


def query_kernel(pieces, columns, place_ref, weights_ref, cos_ref, sin_ref, *refs, scale):
    *arrays, out_ref, total = refs
    accumulated(pieces, columns, place_ref, weights_ref, arrays, total)
    for head in range((columns[1] - columns[0]) // HEAD_DIM):
        part = total[:, head * HEAD_DIM : (head + 1) * HEAD_DIM]
        queries = turned(part, cos_ref[...], sin_ref[...]) * scale
        out_ref[:, head * HEAD_DIM : (head + 1) * HEAD_DIM] = queries.astype(jnp.bfloat16)


def attention_kernel(low_ref, q_ref, far_ref, near_ref, own_ref, grad_ref, att_ref, *refs):
    far_out, near_out, own_out, keys, values, acc = refs
    tokens, width = q_ref.shape
    for number, ref in enumerate((far_ref, near_ref, own_ref)):
        keys[number * tokens : (number + 1) * tokens] = ref[0]
        values[number * tokens : (number + 1) * tokens] = ref[1]
    acc[...] = jnp.zeros_like(acc)
    span = 2 * tokens + BLOCK
    heads = width // HEAD_DIM
    for head in range(heads):
        cols = slice(head * HEAD_DIM, (head + 1) * HEAD_DIM)
        for at in range(0, tokens, BLOCK):
            rows = slice(at, at + BLOCK)
            window = slice(at, at + span)
            low = low_ref[:, rows]
            key_at = lax.broadcasted_iota(jnp.int32, (span, BLOCK), 0) + at
            query_at = lax.broadcasted_iota(jnp.int32, (span, BLOCK), 1) + (2 * tokens + at)
            allowed = (key_at >= low) & (key_at <= query_at)
            query = q_ref[rows, cols]
            grad = grad_ref[rows, cols]
            scores = lax.dot_general(
                keys[window], query, CONTRACT_COLS, preferred_element_type=jnp.float32
            )
            scores = jnp.where(allowed, scores, -jnp.inf)
            raw = jnp.exp(scores - jnp.max(scores, axis=0, keepdims=True))
            probs = raw * (1.0 / jnp.sum(raw, axis=0, keepdims=True))
            low_probs = probs.astype(jnp.bfloat16)
            attended = lax.dot_general(
                values[window], low_probs, CONTRACT_ROWS, preferred_element_type=jnp.float32
            )
            attended = attended.T.astype(jnp.bfloat16)
            att_ref[rows, cols] = attended
            product = grad.astype(jnp.float32) * attended.astype(jnp.float32)
            out_dot = jnp.sum(product.T, axis=0, keepdims=True)
            acc[1, window] += jnp.dot(low_probs, grad, preferred_element_type=jnp.float32)
            prob_grad = lax.dot_general(
                values[window], grad, CONTRACT_COLS, preferred_element_type=jnp.float32
            )
            score_grad = (probs * (prob_grad - out_dot)).astype(jnp.bfloat16)
            acc[0, window] += jnp.dot(score_grad, query, preferred_element_type=jnp.float32)
    far_out[...] = acc[:, :tokens].astype(jnp.bfloat16)
    near_out[...] = acc[:, tokens : 2 * tokens].astype(jnp.bfloat16)
    own_out[...] = acc[:, 2 * tokens :]


def attention_call(low, queries, far, near, own, grads):
    tokens, width = queries.shape
    vmem = pl.BlockSpec(memory_space=pltpu.VMEM)
    block = jax.ShapeDtypeStruct(own.shape, jnp.bfloat16)
    pairs = tokens * (2 * tokens + BLOCK) * (width // HEAD_DIM)
    return pl.pallas_call(
        attention_kernel,
        out_shape=(
            jax.ShapeDtypeStruct((tokens, width), jnp.bfloat16),
            block,
            block,
            jax.ShapeDtypeStruct(own.shape, jnp.float32),
        ),
        in_specs=[vmem] * 6,
        out_specs=(vmem,) * 4,
        scratch_shapes=[
            pltpu.VMEM((3 * tokens, HEAD_DIM), jnp.bfloat16),
            pltpu.VMEM((3 * tokens, HEAD_DIM), jnp.bfloat16),
            pltpu.VMEM((2, 3 * tokens, HEAD_DIM), jnp.float32),
        ],
        compiler_params=pltpu.CompilerParams(vmem_limit_bytes=10 << 20),
        cost_estimate=pl.CostEstimate(
            flops=10 * pairs * HEAD_DIM,
            bytes_accessed=4 * tokens * width * 4,
            transcendentals=pairs,
        ),
        name="attention",
    )(low, queries, far, near, own, grads)


def project(kernel, out_shape, arrays, pieces, columns, place, weights, tables, begun=()):
    tokens = arrays[0].shape[2]
    width = columns[1] - columns[0]
    depth = len(pieces) * arrays[0].shape[1]
    vmem = pl.BlockSpec(memory_space=pltpu.VMEM)
    return pl.pallas_call(
        functools.partial(kernel, pieces, columns),
        out_shape=out_shape,
        in_specs=[pl.BlockSpec(memory_space=pltpu.SMEM)] + [vmem] * (3 + len(arrays) + len(begun)),
        out_specs=vmem,
        scratch_shapes=[pltpu.VMEM((tokens, width), jnp.float32)],
        compiler_params=pltpu.CompilerParams(vmem_limit_bytes=10 << 20),
        cost_estimate=pl.CostEstimate(
            flops=2 * tokens * depth * width,
            bytes_accessed=2 * depth * (tokens + width) + 4 * tokens * width,
            transcendentals=0,
        ),
        name="project",
    )(place, weights, *tables, *arrays, *begun)


def weight_grad_kernel(
    pieces, partner, place_ref, own_ref, near_ref, far_ref, cos_ref, sin_ref, *refs
):
    *arrays, out_ref, grads = refs
    core = place_ref[16]
    wanted = 1 - core if partner else core
    sums = [
        own_ref[i] + near_ref[i].astype(jnp.float32) + far_ref[i].astype(jnp.float32)
        for i in range(2)
    ]
    grads[:, :HEAD_DIM] = unturned(sums[0], cos_ref[...], sin_ref[...]).astype(jnp.bfloat16)
    grads[:, HEAD_DIM:] = sums[1].astype(jnp.bfloat16)
    for array, at, x_step, y_step, half in pieces:
        if half == 0:
            term = jnp.dot(
                arrays[array][at + wanted], grads[...], preferred_element_type=jnp.float32
            )
            out_ref[place_ref[x_step * 4 + y_step]] = term.astype(jnp.bfloat16)


def weight_grad(arrays, pieces, place, own, near, far, tables, partner):
    rows, tokens = arrays[0].shape[1:]
    width = 2 * HEAD_DIM
    vmem = pl.BlockSpec(memory_space=pltpu.VMEM)
    depth = len(pieces) * rows // 2
    return pl.pallas_call(
        functools.partial(weight_grad_kernel, pieces, partner),
        out_shape=jax.ShapeDtypeStruct((16, rows, width), jnp.bfloat16),
        in_specs=[pl.BlockSpec(memory_space=pltpu.SMEM)] + [vmem] * (5 + len(arrays)),
        out_specs=vmem,
        scratch_shapes=[pltpu.VMEM((tokens, width), jnp.bfloat16)],
        compiler_params=pltpu.CompilerParams(vmem_limit_bytes=10 << 20),
        cost_estimate=pl.CostEstimate(
            flops=2 * tokens * depth * width,
            bytes_accessed=2 * depth * (tokens + width) + 2 * tokens * width,
            transcendentals=0,
        ),
        name="weight_grad",
    )(place, own, near, far, *tables, *arrays)


def scattered_sum(kept, sent):
    chip = kept.astype(jnp.float32) + cycled(sent, "core", 1).astype(jnp.float32)
    chip = chip.astype(jnp.bfloat16)
    landed = lax.all_to_all(chip, ("z", "far"), 0, 0, tiled=True)
    return jnp.sum(landed.astype(jnp.float32), axis=0)


def spread_weights(query_weight, key_weight, value_weight):
    own = jnp.concatenate([query_weight, key_weight, value_weight], axis=1)
    other = cycled(own, "far", 1)
    far = lax.axis_index("far")
    both = jnp.where(far == 0, jnp.stack([own, other]), jnp.stack([other, own]))
    return lax.all_gather(both, ("z", "core"), axis=0, tiled=False)


def shards(features, query_weight, key_weight, value_weight, doc_lengths, out_grad):
    tok_rows, slab_rows = features.shape
    query_cols = query_weight.shape[1]
    value_cols = key_weight.shape[1]
    query_scale = (slab_rows * 16 / HEADS_Q) ** (-0.5)
    ctx_index = lax.axis_index(CTX)

    arrays, pieces, early = spread_features(features.T.reshape(2, slab_rows // 2, tok_rows))
    weights = spread_weights(query_weight, key_weight, value_weight)
    step = jnp.arange(4, dtype=jnp.int32)
    x_at, y_at = lax.axis_index("x"), lax.axis_index("y")
    place = ((x_at + step) % 4)[:, None] * 4 + ((y_at + step) % 4)[None, :]
    place = jnp.concatenate([place.reshape(16), jnp.stack([lax.axis_index("core"), y_at])])
    place = place.astype(jnp.int32)

    starts = jnp.cumsum(doc_lengths) - doc_lengths
    query_index = ctx_index * tok_rows + jnp.arange(tok_rows, dtype=jnp.int32)
    query_start = start_of(query_index, starts)
    tables = rope_tables(query_index - query_start)
    low = jnp.maximum(query_start, query_index - (WINDOW - 1)) - (ctx_index - SPAN) * tok_rows
    low = low.astype(jnp.int32)[None]

    columns = (query_cols, query_cols + 2 * value_cols)
    begun = project(
        partial_kernel,
        jax.ShapeDtypeStruct((tok_rows, 2 * value_cols), jnp.float32),
        arrays[:early],
        [piece for piece in pieces if piece[0] < early],
        columns,
        place,
        weights,
        tables,
    )
    key_value = project(
        key_value_kernel,
        jax.ShapeDtypeStruct((2, tok_rows, HEAD_DIM), jnp.bfloat16),
        arrays[early:],
        [(piece[0] - early, *piece[1:]) for piece in pieces if piece[0] >= early],
        columns,
        place,
        weights,
        tables,
        (begun,),
    )
    far, near = passed_along(key_value, 2), passed_along(key_value, 1)
    queries = project(
        functools.partial(query_kernel, scale=query_scale),
        jax.ShapeDtypeStruct((tok_rows, query_cols), jnp.bfloat16),
        arrays,
        pieces,
        (0, query_cols),
        place,
        weights,
        tables,
    )
    attention, far_part, near_part, own_part = attention_call(
        low, queries, far, near, key_value, out_grad
    )
    far_back, near_back = passed_along(far_part, -2), passed_along(near_part, -1)
    sent, kept = (
        weight_grad(arrays, pieces, place, own_part, near_back, far_back, tables, partner)
        for partner in (True, False)
    )
    weight_grads = scattered_sum(kept, sent).astype(jnp.bfloat16)
    return attention, weight_grads[:, :value_cols], weight_grads[:, value_cols:]


def solution(mesh):
    sizes = (mesh.shape["ctx"] // 4, 2, 2, 4, 4)
    torus = Mesh(mesh.devices.reshape(sizes), CTX + HEAD)
    placed = (P(CTX, HEAD), P(CTX, HEAD), P(CTX, HEAD), P(CTX, HEAD), P(), P(CTX, HEAD))
    return jax.shard_map(
        shards,
        mesh=torus,
        in_specs=placed,
        out_specs=(P(CTX, HEAD), P(CTX, HEAD), P(CTX, HEAD)),
        check_vma=False,
    )
```

```python
import functools

import jax
import jax.numpy as jnp
from jax import lax
from jax.experimental import pallas as pl
from jax.experimental.pallas import tpu as pltpu
from jax.sharding import Mesh
from jax.sharding import PartitionSpec as P


HEADS_Q = 32
HEAD_DIM = 128
WINDOW = 1024
SPAN = 2
CORES = 2
CTX = ("z", "far", "core")
HEAD = ("x", "y")
ROPE_BASE = 10000.0


def cycled(value, axis, step):
    count = lax.axis_size(axis)
    return lax.ppermute(value, axis, [(i, (i + step) % count) for i in range(count)])


def passed_along(block, distance):
    devices = range(lax.axis_size(CTX))
    route = [(i - distance, i) for i in devices if i - distance in devices]
    return lax.ppermute(block, CTX, route)


def rope_tables(offsets):
    middle = HEAD_DIM // 2
    inverse = ROPE_BASE ** (-(jnp.arange(middle).astype(jnp.float32) * 2.0 / HEAD_DIM))
    angles = offsets.astype(jnp.float32)[:, None] * inverse[None, :]
    cosine = jnp.cos(angles)
    sine = jnp.sin(angles)
    return (
        jnp.concatenate([cosine, cosine], axis=-1),
        jnp.concatenate([-sine, sine], axis=-1),
    )


def start_of(positions, starts):
    candidates = jnp.where(starts[None, :] <= positions[:, None], starts[None, :], -1)
    return jnp.max(candidates, axis=1)


def spread_features(own):
    arrays, pieces = [], []

    def add(array, entries):
        for at, (x_step, y_step, half) in enumerate(entries):
            pieces.append((len(arrays), at, x_step, y_step, half))
        arrays.append(array)

    def across(batch, y_steps, x_steps):
        halves = [(y_step, half) for y_step in y_steps for half in range(2)]
        add(batch, [(0, *entry) for entry in halves])
        for x_step in x_steps:
            moved = cycled(batch, "x", -x_step)
            add(moved, [(x_step, *entry) for entry in halves])

    above = cycled(own, "y", 1)
    below = cycled(own, "y", -1)
    across(own, (0,), (1, 3, 2))
    sides = jnp.concatenate([above, below])
    across(sides, (3, 1), (1, 3))
    early = len(arrays)
    opposite = cycled(own, "y", 2)
    across(opposite, (2,), (1, 3, 2))
    right, left = arrays[early - 2 : early]
    for moved, x_shift, y_step in ((left[:2], 1, 3), (right[2:], -1, 1)):
        moved = cycled(moved, "x", x_shift)
        add(moved, [(2, y_step, 0), (2, y_step, 1)])
    return arrays, pieces, early


CONTRACT_ROWS = (((0,), (0,)), ((), ()))
CONTRACT_COLS = (((1,), (1,)), ((), ()))
BLOCK = 256


def turned(values, cosine, sine_signed):
    return values * cosine + pltpu.roll(values, HEAD_DIM // 2, 1) * sine_signed


def unturned(values, cosine, sine_signed):
    return values * cosine - pltpu.roll(values, HEAD_DIM // 2, 1) * sine_signed


def accumulated(pieces, columns, place_ref, weights_ref, arrays, total, begun=None):
    first, last = columns
    for number, (array, at, x_step, y_step, half) in enumerate(pieces):
        place = place_ref[x_step * 4 + y_step]
        weight = weights_ref[(place // 2) * CORES + half, place % 2, :, first:last]
        term = lax.dot_general(
            arrays[array][at], weight, CONTRACT_ROWS, preferred_element_type=jnp.float32
        )
        if number == 0:
            total[...] = term if begun is None else begun[...] + term
        else:
            total[...] += term


def partial_kernel(pieces, columns, place_ref, weights_ref, cos_ref, sin_ref, *refs):
    *arrays, out_ref, total = refs
    accumulated(pieces, columns, place_ref, weights_ref, arrays, total)
    out_ref[...] = total[...]


def key_value_kernel(pieces, columns, place_ref, weights_ref, cos_ref, sin_ref, *refs):
    *arrays, begun, out_ref, total = refs
    accumulated(pieces, columns, place_ref, weights_ref, arrays, total, begun)
    keys = turned(total[:, :HEAD_DIM], cos_ref[...], sin_ref[...])
    out_ref[0] = keys.astype(jnp.bfloat16)
    out_ref[1] = total[:, HEAD_DIM:].astype(jnp.bfloat16)


def query_kernel(pieces, columns, place_ref, weights_ref, cos_ref, sin_ref, *refs, scale):
    *arrays, out_ref, total = refs
    accumulated(pieces, columns, place_ref, weights_ref, arrays, total)
    for head in range((columns[1] - columns[0]) // HEAD_DIM):
        part = total[:, head * HEAD_DIM : (head + 1) * HEAD_DIM]
        queries = turned(part, cos_ref[...], sin_ref[...]) * scale
        out_ref[:, head * HEAD_DIM : (head + 1) * HEAD_DIM] = queries.astype(jnp.bfloat16)


def attention_kernel(low_ref, q_ref, far_ref, near_ref, own_ref, grad_ref, *refs):
    att_ref, probs_ref, dot_ref, far_out, near_out, own_out, keys, values, acc = refs
    tokens, width = q_ref.shape
    for number, ref in enumerate((far_ref, near_ref, own_ref)):
        keys[number * tokens : (number + 1) * tokens] = ref[0]
        values[number * tokens : (number + 1) * tokens] = ref[1]
    acc[...] = jnp.zeros_like(acc)
    span = 2 * tokens + BLOCK
    tiles = [(head, at) for head in range(width // HEAD_DIM) for at in range(0, tokens, BLOCK)]
    for number, (head, at) in enumerate(tiles):
        cols = slice(head * HEAD_DIM, (head + 1) * HEAD_DIM)
        rows = slice(at, at + BLOCK)
        window = slice(at, at + span)
        low = low_ref[:, rows]
        key_at = lax.broadcasted_iota(jnp.int32, (span, BLOCK), 0) + at
        query_at = lax.broadcasted_iota(jnp.int32, (span, BLOCK), 1) + (2 * tokens + at)
        allowed = (key_at >= low) & (key_at <= query_at)
        grad = grad_ref[rows, cols]
        scores = lax.dot_general(
            keys[window], q_ref[rows, cols], CONTRACT_COLS, preferred_element_type=jnp.float32
        )
        scores = jnp.where(allowed, scores, -jnp.inf)
        raw = jnp.exp(scores - jnp.max(scores, axis=0, keepdims=True))
        probs = raw * (1.0 / jnp.sum(raw, axis=0, keepdims=True))
        probs_ref[number] = probs
        low_probs = probs.astype(jnp.bfloat16)
        acc[window] += jnp.dot(low_probs, grad, preferred_element_type=jnp.float32)
        attended = lax.dot_general(
            values[window], low_probs, CONTRACT_ROWS, preferred_element_type=jnp.float32
        )
        attended = attended.T.astype(jnp.bfloat16)
        att_ref[rows, cols] = attended
        product = grad.astype(jnp.float32) * attended.astype(jnp.float32)
        dot_ref[number] = jnp.sum(product.T, axis=0, keepdims=True)
    far_out[...] = acc[:tokens].astype(jnp.bfloat16)
    near_out[...] = acc[tokens : 2 * tokens].astype(jnp.bfloat16)
    own_out[...] = acc[2 * tokens :]


def key_grad_kernel(probs_ref, dot_ref, q_ref, far_ref, near_ref, own_ref, grad_ref, *refs):
    far_out, near_out, own_out, values, acc = refs
    tokens, width = q_ref.shape
    for number, ref in enumerate((far_ref, near_ref, own_ref)):
        values[number * tokens : (number + 1) * tokens] = ref[1]
    acc[...] = jnp.zeros_like(acc)
    span = 2 * tokens + BLOCK
    tiles = [(head, at) for head in range(width // HEAD_DIM) for at in range(0, tokens, BLOCK)]
    for number, (head, at) in enumerate(tiles):
        cols = slice(head * HEAD_DIM, (head + 1) * HEAD_DIM)
        rows = slice(at, at + BLOCK)
        window = slice(at, at + span)
        prob_grad = lax.dot_general(
            values[window], grad_ref[rows, cols], CONTRACT_COLS, preferred_element_type=jnp.float32
        )
        score_grad = (probs_ref[number] * (prob_grad - dot_ref[number])).astype(jnp.bfloat16)
        acc[window] += jnp.dot(score_grad, q_ref[rows, cols], preferred_element_type=jnp.float32)
    far_out[...] = acc[:tokens].astype(jnp.bfloat16)
    near_out[...] = acc[tokens : 2 * tokens].astype(jnp.bfloat16)
    own_out[...] = acc[2 * tokens :]


def attention_calls(low, queries, far, near, own, grads):
    tokens, width = queries.shape
    vmem = pl.BlockSpec(memory_space=pltpu.VMEM)
    tiles = (width // HEAD_DIM) * (tokens // BLOCK)
    span = 2 * tokens + BLOCK
    part = jax.ShapeDtypeStruct((tokens, HEAD_DIM), jnp.bfloat16)
    parts = (part, part, jax.ShapeDtypeStruct((tokens, HEAD_DIM), jnp.float32))
    block = pltpu.VMEM((3 * tokens, HEAD_DIM), jnp.bfloat16)
    total = pltpu.VMEM((3 * tokens, HEAD_DIM), jnp.float32)
    pairs = tiles * span * BLOCK
    attention, probs, dots, *value_parts = pl.pallas_call(
        attention_kernel,
        out_shape=(
            jax.ShapeDtypeStruct((tokens, width), jnp.bfloat16),
            jax.ShapeDtypeStruct((tiles, span, BLOCK), jnp.float32),
            jax.ShapeDtypeStruct((tiles, 1, BLOCK), jnp.float32),
            *parts,
        ),
        in_specs=[vmem] * 6,
        out_specs=(vmem,) * 6,
        scratch_shapes=[block, block, total],
        compiler_params=pltpu.CompilerParams(vmem_limit_bytes=14 << 20),
        cost_estimate=pl.CostEstimate(
            flops=6 * pairs * HEAD_DIM, bytes_accessed=8 * tokens * width, transcendentals=pairs
        ),
        name="attention",
    )(low, queries, far, near, own, grads)
    key_parts = pl.pallas_call(
        key_grad_kernel,
        out_shape=parts,
        in_specs=[vmem] * 7,
        out_specs=(vmem,) * 3,
        scratch_shapes=[block, total],
        compiler_params=pltpu.CompilerParams(vmem_limit_bytes=14 << 20),
        cost_estimate=pl.CostEstimate(
            flops=4 * pairs * HEAD_DIM, bytes_accessed=8 * tokens * width, transcendentals=0
        ),
        name="key_grad",
    )(probs, dots, queries, far, near, own, grads)
    return attention, key_parts, value_parts


def project(kernel, out_shape, arrays, pieces, columns, place, weights, tables, begun=()):
    tokens = arrays[0].shape[2]
    width = columns[1] - columns[0]
    depth = len(pieces) * arrays[0].shape[1]
    vmem = pl.BlockSpec(memory_space=pltpu.VMEM)
    return pl.pallas_call(
        functools.partial(kernel, pieces, columns),
        out_shape=out_shape,
        in_specs=[pl.BlockSpec(memory_space=pltpu.SMEM)] + [vmem] * (3 + len(arrays) + len(begun)),
        out_specs=vmem,
        scratch_shapes=[pltpu.VMEM((tokens, width), jnp.float32)],
        compiler_params=pltpu.CompilerParams(vmem_limit_bytes=10 << 20),
        cost_estimate=pl.CostEstimate(
            flops=2 * tokens * depth * width,
            bytes_accessed=2 * depth * (tokens + width) + 4 * tokens * width,
            transcendentals=0,
        ),
        name="project",
    )(place, weights, *tables, *arrays, *begun)


def weight_grad_kernel(pieces, partner, place_ref, *refs):
    parts, (cos_ref, sin_ref, *arrays, out_ref, grads) = refs[:6], refs[6:]
    core = place_ref[16]
    wanted = 1 - core if partner else core
    sums = [
        own[...] + near[...].astype(jnp.float32) + far[...].astype(jnp.float32)
        for own, near, far in (parts[:3], parts[3:])
    ]
    grads[:, :HEAD_DIM] = unturned(sums[0], cos_ref[...], sin_ref[...]).astype(jnp.bfloat16)
    grads[:, HEAD_DIM:] = sums[1].astype(jnp.bfloat16)
    for array, at, x_step, y_step, half in pieces:
        if half == 0:
            term = jnp.dot(
                arrays[array][at + wanted], grads[...], preferred_element_type=jnp.float32
            )
            out_ref[place_ref[x_step * 4 + y_step]] = term.astype(jnp.bfloat16)


def weight_grad(arrays, pieces, place, parts, tables, partner):
    rows, tokens = arrays[0].shape[1:]
    width = 2 * HEAD_DIM
    vmem = pl.BlockSpec(memory_space=pltpu.VMEM)
    depth = len(pieces) * rows // 2
    return pl.pallas_call(
        functools.partial(weight_grad_kernel, pieces, partner),
        out_shape=jax.ShapeDtypeStruct((16, rows, width), jnp.bfloat16),
        in_specs=[pl.BlockSpec(memory_space=pltpu.SMEM)] + [vmem] * (8 + len(arrays)),
        out_specs=vmem,
        scratch_shapes=[pltpu.VMEM((tokens, width), jnp.bfloat16)],
        compiler_params=pltpu.CompilerParams(vmem_limit_bytes=10 << 20),
        cost_estimate=pl.CostEstimate(
            flops=2 * tokens * depth * width,
            bytes_accessed=2 * depth * (tokens + width) + 2 * tokens * width,
            transcendentals=0,
        ),
        name="weight_grad",
    )(place, *parts, *tables, *arrays)


def scattered_sum(kept, sent):
    chip = kept.astype(jnp.float32) + cycled(sent, "core", 1).astype(jnp.float32)
    chip = chip.astype(jnp.bfloat16)
    landed = lax.all_to_all(chip, ("z", "far"), 0, 0, tiled=True)
    return jnp.sum(landed.astype(jnp.float32), axis=0)


def spread_weights(query_weight, key_weight, value_weight):
    own = jnp.concatenate([query_weight, key_weight, value_weight], axis=1)
    other = cycled(own, "far", 1)
    far = lax.axis_index("far")
    both = jnp.where(far == 0, jnp.stack([own, other]), jnp.stack([other, own]))
    return lax.all_gather(both, ("z", "core"), axis=0, tiled=False)


def shards(features, query_weight, key_weight, value_weight, doc_lengths, out_grad):
    tok_rows, slab_rows = features.shape
    query_cols = query_weight.shape[1]
    value_cols = key_weight.shape[1]
    query_scale = (slab_rows * 16 / HEADS_Q) ** (-0.5)
    ctx_index = lax.axis_index(CTX)

    arrays, pieces, early = spread_features(features.T.reshape(2, slab_rows // 2, tok_rows))
    weights = spread_weights(query_weight, key_weight, value_weight)
    step = jnp.arange(4, dtype=jnp.int32)
    x_at, y_at = lax.axis_index("x"), lax.axis_index("y")
    place = ((x_at + step) % 4)[:, None] * 4 + ((y_at + step) % 4)[None, :]
    place = jnp.concatenate([place.reshape(16), jnp.stack([lax.axis_index("core"), y_at])])
    place = place.astype(jnp.int32)

    starts = jnp.cumsum(doc_lengths) - doc_lengths
    query_index = ctx_index * tok_rows + jnp.arange(tok_rows, dtype=jnp.int32)
    query_start = start_of(query_index, starts)
    tables = rope_tables(query_index - query_start)
    low = jnp.maximum(query_start, query_index - (WINDOW - 1)) - (ctx_index - SPAN) * tok_rows
    low = low.astype(jnp.int32)[None]

    columns = (query_cols, query_cols + 2 * value_cols)
    begun = project(
        partial_kernel,
        jax.ShapeDtypeStruct((tok_rows, 2 * value_cols), jnp.float32),
        arrays[:early],
        [piece for piece in pieces if piece[0] < early],
        columns,
        place,
        weights,
        tables,
    )
    key_value = project(
        key_value_kernel,
        jax.ShapeDtypeStruct((2, tok_rows, HEAD_DIM), jnp.bfloat16),
        arrays[early:],
        [(piece[0] - early, *piece[1:]) for piece in pieces if piece[0] >= early],
        columns,
        place,
        weights,
        tables,
        (begun,),
    )
    far, near = passed_along(key_value, 2), passed_along(key_value, 1)
    queries = project(
        functools.partial(query_kernel, scale=query_scale),
        jax.ShapeDtypeStruct((tok_rows, query_cols), jnp.bfloat16),
        arrays,
        pieces,
        (0, query_cols),
        place,
        weights,
        tables,
    )
    attention, key_parts, value_parts = attention_calls(
        low, queries, far, near, key_value, out_grad
    )
    back = []
    for (far_part, near_part, own_part) in (value_parts, key_parts):
        far_back = passed_along(far_part, -2)
        near_back = passed_along(near_part, -1)
        back.append((own_part, near_back, far_back))
    sent, kept = (
        weight_grad(arrays, pieces, place, back[1] + back[0], tables, partner)
        for partner in (True, False)
    )
    weight_grads = scattered_sum(kept, sent).astype(jnp.bfloat16)
    return attention, weight_grads[:, :value_cols], weight_grads[:, value_cols:]


def solution(mesh):
    sizes = (mesh.shape["ctx"] // 4, 2, 2, 4, 4)
    torus = Mesh(mesh.devices.reshape(sizes), CTX + HEAD)
    placed = (P(CTX, HEAD), P(CTX, HEAD), P(CTX, HEAD), P(CTX, HEAD), P(), P(CTX, HEAD))
    return jax.shard_map(
        shards,
        mesh=torus,
        in_specs=placed,
        out_specs=(P(CTX, HEAD), P(CTX, HEAD), P(CTX, HEAD)),
        check_vma=False,
    )
```

```python
import functools

import jax
import jax.numpy as jnp
from jax import lax
from jax.experimental import pallas as pl
from jax.experimental.pallas import tpu as pltpu
from jax.sharding import Mesh
from jax.sharding import PartitionSpec as P


HEADS_Q = 32
HEAD_DIM = 128
WINDOW = 1024
SPAN = 2
CORES = 2
CTX = ("z", "far", "core")
HEAD = ("x", "y")
ROPE_BASE = 10000.0


def cycled(value, axis, step):
    count = lax.axis_size(axis)
    return lax.ppermute(value, axis, [(i, (i + step) % count) for i in range(count)])


def passed_along(block, distance):
    devices = range(lax.axis_size(CTX))
    route = [(i - distance, i) for i in devices if i - distance in devices]
    return lax.ppermute(block, CTX, route)


def rope_tables(offsets):
    middle = HEAD_DIM // 2
    inverse = ROPE_BASE ** (-(jnp.arange(middle).astype(jnp.float32) * 2.0 / HEAD_DIM))
    angles = offsets.astype(jnp.float32)[:, None] * inverse[None, :]
    cosine = jnp.cos(angles)
    sine = jnp.sin(angles)
    return (
        jnp.concatenate([cosine, cosine], axis=-1),
        jnp.concatenate([-sine, sine], axis=-1),
    )


def start_of(positions, starts):
    candidates = jnp.where(starts[None, :] <= positions[:, None], starts[None, :], -1)
    return jnp.max(candidates, axis=1)


def spread_features(own):
    arrays, pieces = [], []

    def add(array, entries):
        for at, (x_step, y_step, half) in enumerate(entries):
            pieces.append((len(arrays), at, x_step, y_step, half))
        arrays.append(array)

    def across(batch, y_steps, x_steps):
        halves = [(y_step, half) for y_step in y_steps for half in range(2)]
        add(batch, [(0, *entry) for entry in halves])
        for x_step in x_steps:
            moved = cycled(batch, "x", -x_step)
            add(moved, [(x_step, *entry) for entry in halves])

    above = cycled(own, "y", 1)
    below = cycled(own, "y", -1)
    across(own, (0,), (1, 3, 2))
    sides = jnp.concatenate([above, below])
    across(sides, (3, 1), (1, 3))
    early = len(arrays)
    opposite = cycled(own, "y", 2)
    across(opposite, (2,), (1, 3, 2))
    right, left = arrays[early - 2 : early]
    for moved, x_shift, y_step in ((left[:2], 1, 3), (right[2:], -1, 1)):
        moved = cycled(moved, "x", x_shift)
        add(moved, [(2, y_step, 0), (2, y_step, 1)])
    return arrays, pieces, early


CONTRACT_ROWS = (((0,), (0,)), ((), ()))
CONTRACT_COLS = (((1,), (1,)), ((), ()))
BLOCK = 256


def turned(values, cosine, sine_signed):
    return values * cosine + pltpu.roll(values, HEAD_DIM // 2, 1) * sine_signed


def unturned(values, cosine, sine_signed):
    return values * cosine - pltpu.roll(values, HEAD_DIM // 2, 1) * sine_signed


def accumulated(pieces, columns, place_ref, weights_ref, arrays, total, begun=None):
    first, last = columns
    for number, (array, at, x_step, y_step, half) in enumerate(pieces):
        place = place_ref[x_step * 4 + y_step]
        weight = weights_ref[(place // 2) * CORES + half, place % 2, :, first:last]
        term = lax.dot_general(
            arrays[array][at], weight, CONTRACT_ROWS, preferred_element_type=jnp.float32
        )
        if number == 0:
            total[...] = term if begun is None else begun[...] + term
        else:
            total[...] += term


def partial_kernel(pieces, columns, place_ref, weights_ref, cos_ref, sin_ref, *refs):
    *arrays, out_ref, total = refs
    accumulated(pieces, columns, place_ref, weights_ref, arrays, total)
    out_ref[...] = total[...]


def key_value_kernel(pieces, columns, place_ref, weights_ref, cos_ref, sin_ref, *refs):
    *arrays, begun, out_ref, total = refs
    accumulated(pieces, columns, place_ref, weights_ref, arrays, total, begun)
    keys = turned(total[:, :HEAD_DIM], cos_ref[...], sin_ref[...])
    out_ref[0] = keys.astype(jnp.bfloat16)
    out_ref[1] = total[:, HEAD_DIM:].astype(jnp.bfloat16)


def query_kernel(pieces, columns, place_ref, weights_ref, cos_ref, sin_ref, *refs, scale):
    *arrays, out_ref, total = refs
    accumulated(pieces, columns, place_ref, weights_ref, arrays, total)
    for head in range((columns[1] - columns[0]) // HEAD_DIM):
        part = total[:, head * HEAD_DIM : (head + 1) * HEAD_DIM]
        queries = turned(part, cos_ref[...], sin_ref[...]) * scale
        out_ref[:, head * HEAD_DIM : (head + 1) * HEAD_DIM] = queries.astype(jnp.bfloat16)


def attention_kernel(low_ref, q_ref, far_ref, near_ref, own_ref, grad_ref, att_ref, *refs):
    far_out, near_out, own_out, keys, values, acc = refs
    tokens, width = q_ref.shape
    for number, ref in enumerate((far_ref, near_ref, own_ref)):
        keys[number * tokens : (number + 1) * tokens] = ref[0]
        values[number * tokens : (number + 1) * tokens] = ref[1]
    acc[...] = jnp.zeros_like(acc)
    span = 2 * tokens + BLOCK
    heads = width // HEAD_DIM
    for head in range(heads):
        cols = slice(head * HEAD_DIM, (head + 1) * HEAD_DIM)
        for at in range(0, tokens, BLOCK):
            rows = slice(at, at + BLOCK)
            window = slice(at, at + span)
            low = low_ref[:, rows]
            key_at = lax.broadcasted_iota(jnp.int32, (span, BLOCK), 0) + at
            query_at = lax.broadcasted_iota(jnp.int32, (span, BLOCK), 1) + (2 * tokens + at)
            allowed = (key_at >= low) & (key_at <= query_at)
            query = q_ref[rows, cols]
            grad = grad_ref[rows, cols]
            scores = lax.dot_general(
                keys[window], query, CONTRACT_COLS, preferred_element_type=jnp.float32
            )
            scores = jnp.where(allowed, scores, -jnp.inf)
            raw = jnp.exp(scores - jnp.max(scores, axis=0, keepdims=True))
            probs = raw * (1.0 / jnp.sum(raw, axis=0, keepdims=True))
            low_probs = probs.astype(jnp.bfloat16)
            attended = lax.dot_general(
                values[window], low_probs, CONTRACT_ROWS, preferred_element_type=jnp.float32
            )
            attended = attended.T.astype(jnp.bfloat16)
            att_ref[rows, cols] = attended
            product = grad.astype(jnp.float32) * attended.astype(jnp.float32)
            out_dot = jnp.sum(product.T, axis=0, keepdims=True)
            acc[1, window] += jnp.dot(low_probs, grad, preferred_element_type=jnp.float32)
            prob_grad = lax.dot_general(
                values[window], grad, CONTRACT_COLS, preferred_element_type=jnp.float32
            )
            score_grad = (probs * (prob_grad - out_dot)).astype(jnp.bfloat16)
            acc[0, window] += jnp.dot(score_grad, query, preferred_element_type=jnp.float32)
    far_out[...] = acc[:, :tokens].astype(jnp.bfloat16)
    near_out[...] = acc[:, tokens : 2 * tokens].astype(jnp.bfloat16)
    own_out[...] = acc[:, 2 * tokens :]


def attention_call(low, queries, far, near, own, grads):
    tokens, width = queries.shape
    vmem = pl.BlockSpec(memory_space=pltpu.VMEM)
    block = jax.ShapeDtypeStruct(own.shape, jnp.bfloat16)
    pairs = tokens * (2 * tokens + BLOCK) * (width // HEAD_DIM)
    return pl.pallas_call(
        attention_kernel,
        out_shape=(
            jax.ShapeDtypeStruct((tokens, width), jnp.bfloat16),
            block,
            block,
            jax.ShapeDtypeStruct(own.shape, jnp.float32),
        ),
        in_specs=[vmem] * 6,
        out_specs=(vmem,) * 4,
        scratch_shapes=[
            pltpu.VMEM((3 * tokens, HEAD_DIM), jnp.bfloat16),
            pltpu.VMEM((3 * tokens, HEAD_DIM), jnp.bfloat16),
            pltpu.VMEM((2, 3 * tokens, HEAD_DIM), jnp.float32),
        ],
        compiler_params=pltpu.CompilerParams(vmem_limit_bytes=10 << 20),
        cost_estimate=pl.CostEstimate(
            flops=10 * pairs * HEAD_DIM,
            bytes_accessed=4 * tokens * width * 4,
            transcendentals=pairs,
        ),
        name="attention",
    )(low, queries, far, near, own, grads)


def project(kernel, out_shape, arrays, pieces, columns, place, weights, tables, begun=()):
    tokens = arrays[0].shape[2]
    width = columns[1] - columns[0]
    depth = len(pieces) * arrays[0].shape[1]
    vmem = pl.BlockSpec(memory_space=pltpu.VMEM)
    return pl.pallas_call(
        functools.partial(kernel, pieces, columns),
        out_shape=out_shape,
        in_specs=[pl.BlockSpec(memory_space=pltpu.SMEM)] + [vmem] * (3 + len(arrays) + len(begun)),
        out_specs=vmem,
        scratch_shapes=[pltpu.VMEM((tokens, width), jnp.float32)],
        compiler_params=pltpu.CompilerParams(vmem_limit_bytes=10 << 20),
        cost_estimate=pl.CostEstimate(
            flops=2 * tokens * depth * width,
            bytes_accessed=2 * depth * (tokens + width) + 4 * tokens * width,
            transcendentals=0,
        ),
        name="project",
    )(place, weights, *tables, *arrays, *begun)


def weight_grad_kernel(
    pieces, partner, place_ref, own_ref, near_ref, far_ref, cos_ref, sin_ref, *refs
):
    *arrays, out_ref, grads = refs
    core = place_ref[16]
    wanted = 1 - core if partner else core
    sums = [
        own_ref[i]
        + jnp.where(core == 0, near_ref[i].astype(jnp.float32), 0.0)
        + far_ref[i].astype(jnp.float32)
        for i in range(2)
    ]
    grads[:, :HEAD_DIM] = unturned(sums[0], cos_ref[...], sin_ref[...]).astype(jnp.bfloat16)
    grads[:, HEAD_DIM:] = sums[1].astype(jnp.bfloat16)
    for array, at, x_step, y_step, half in pieces:
        if half == 0:
            term = jnp.dot(
                arrays[array][at + wanted], grads[...], preferred_element_type=jnp.float32
            )
            out_ref[place_ref[x_step * 4 + y_step]] = term.astype(jnp.bfloat16)


def weight_grad(arrays, pieces, place, own, near, far, tables, partner):
    rows, tokens = arrays[0].shape[1:]
    width = 2 * HEAD_DIM
    vmem = pl.BlockSpec(memory_space=pltpu.VMEM)
    depth = len(pieces) * rows // 2
    return pl.pallas_call(
        functools.partial(weight_grad_kernel, pieces, partner),
        out_shape=jax.ShapeDtypeStruct((16, rows, width), jnp.bfloat16),
        in_specs=[pl.BlockSpec(memory_space=pltpu.SMEM)] + [vmem] * (5 + len(arrays)),
        out_specs=vmem,
        scratch_shapes=[pltpu.VMEM((tokens, width), jnp.bfloat16)],
        compiler_params=pltpu.CompilerParams(vmem_limit_bytes=10 << 20),
        cost_estimate=pl.CostEstimate(
            flops=2 * tokens * depth * width,
            bytes_accessed=2 * depth * (tokens + width) + 2 * tokens * width,
            transcendentals=0,
        ),
        name="weight_grad",
    )(place, own, near, far, *tables, *arrays)


def scattered_sum(kept, sent):
    chip = kept.astype(jnp.float32) + cycled(sent, "core", 1).astype(jnp.float32)
    chip = chip.astype(jnp.bfloat16)
    landed = lax.all_to_all(chip, ("z", "far"), 0, 0, tiled=True)
    return jnp.sum(landed.astype(jnp.float32), axis=0)


def spread_weights(query_weight, key_weight, value_weight):
    own = jnp.concatenate([query_weight, key_weight, value_weight], axis=1)
    other = cycled(own, "far", 1)
    far = lax.axis_index("far")
    both = jnp.where(far == 0, jnp.stack([own, other]), jnp.stack([other, own]))
    return lax.all_gather(both, ("z", "core"), axis=0, tiled=False)


def shards(features, query_weight, key_weight, value_weight, doc_lengths, out_grad):
    tok_rows, slab_rows = features.shape
    query_cols = query_weight.shape[1]
    value_cols = key_weight.shape[1]
    query_scale = (slab_rows * 16 / HEADS_Q) ** (-0.5)
    ctx_index = lax.axis_index(CTX)

    arrays, pieces, early = spread_features(features.T.reshape(2, slab_rows // 2, tok_rows))
    weights = spread_weights(query_weight, key_weight, value_weight)
    step = jnp.arange(4, dtype=jnp.int32)
    x_at, y_at = lax.axis_index("x"), lax.axis_index("y")
    place = ((x_at + step) % 4)[:, None] * 4 + ((y_at + step) % 4)[None, :]
    place = jnp.concatenate([place.reshape(16), jnp.stack([lax.axis_index("core"), y_at])])
    place = place.astype(jnp.int32)

    starts = jnp.cumsum(doc_lengths) - doc_lengths
    query_index = ctx_index * tok_rows + jnp.arange(tok_rows, dtype=jnp.int32)
    query_start = start_of(query_index, starts)
    tables = rope_tables(query_index - query_start)
    low = jnp.maximum(query_start, query_index - (WINDOW - 1)) - (ctx_index - SPAN) * tok_rows
    low = low.astype(jnp.int32)[None]

    columns = (query_cols, query_cols + 2 * value_cols)
    begun = project(
        partial_kernel,
        jax.ShapeDtypeStruct((tok_rows, 2 * value_cols), jnp.float32),
        arrays[:early],
        [piece for piece in pieces if piece[0] < early],
        columns,
        place,
        weights,
        tables,
    )
    key_value = project(
        key_value_kernel,
        jax.ShapeDtypeStruct((2, tok_rows, HEAD_DIM), jnp.bfloat16),
        arrays[early:],
        [(piece[0] - early, *piece[1:]) for piece in pieces if piece[0] >= early],
        columns,
        place,
        weights,
        tables,
        (begun,),
    )
    core = lax.axis_index("core")
    far = passed_along(key_value, CORES)
    near = cycled(jnp.where(core == 0, key_value, far), "core", 1)
    queries = project(
        functools.partial(query_kernel, scale=query_scale),
        jax.ShapeDtypeStruct((tok_rows, query_cols), jnp.bfloat16),
        arrays,
        pieces,
        (0, query_cols),
        place,
        weights,
        tables,
    )
    attention, far_part, near_part, own_part = attention_call(
        low, queries, far, near, key_value, out_grad
    )
    near_back = cycled(near_part, "core", 1)
    joined = far_part.astype(jnp.float32) + near_back.astype(jnp.float32)
    far_back = passed_along(jnp.where(core == 0, far_part, joined.astype(jnp.bfloat16)), -CORES)
    sent, kept = (
        weight_grad(arrays, pieces, place, own_part, near_back, far_back, tables, partner)
        for partner in (True, False)
    )
    weight_grads = scattered_sum(kept, sent).astype(jnp.bfloat16)
    return attention, weight_grads[:, :value_cols], weight_grads[:, value_cols:]


def solution(mesh):
    sizes = (mesh.shape["ctx"] // 4, 2, 2, 4, 4)
    torus = Mesh(mesh.devices.reshape(sizes), CTX + HEAD)
    placed = (P(CTX, HEAD), P(CTX, HEAD), P(CTX, HEAD), P(CTX, HEAD), P(), P(CTX, HEAD))
    return jax.shard_map(
        shards,
        mesh=torus,
        in_specs=placed,
        out_specs=(P(CTX, HEAD), P(CTX, HEAD), P(CTX, HEAD)),
        check_vma=False,
    )
```

```python
import functools

import jax
import jax.numpy as jnp
from jax import lax
from jax.experimental import pallas as pl
from jax.experimental.pallas import tpu as pltpu
from jax.sharding import Mesh
from jax.sharding import PartitionSpec as P


HEADS_Q = 32
HEAD_DIM = 128
WINDOW = 1024
SPAN = 2
CORES = 2
CTX = ("z", "far", "core")
HEAD = ("x", "y")
ROPE_BASE = 10000.0


def cycled(value, axis, step):
    count = lax.axis_size(axis)
    return lax.ppermute(value, axis, [(i, (i + step) % count) for i in range(count)])


def passed_along(block, distance):
    devices = range(lax.axis_size(CTX))
    route = [(i - distance, i) for i in devices if i - distance in devices]
    return lax.ppermute(block, CTX, route)


def rope_tables(offsets):
    middle = HEAD_DIM // 2
    inverse = ROPE_BASE ** (-(jnp.arange(middle).astype(jnp.float32) * 2.0 / HEAD_DIM))
    angles = offsets.astype(jnp.float32)[:, None] * inverse[None, :]
    cosine = jnp.cos(angles)
    sine = jnp.sin(angles)
    return (
        jnp.concatenate([cosine, cosine], axis=-1),
        jnp.concatenate([-sine, sine], axis=-1),
    )


def start_of(positions, starts):
    candidates = jnp.where(starts[None, :] <= positions[:, None], starts[None, :], -1)
    return jnp.max(candidates, axis=1)


def spread_features(own):
    arrays, pieces = [], []

    def add(array, entries):
        for at, (x_step, y_step, half) in enumerate(entries):
            pieces.append((len(arrays), at, x_step, y_step, half))
        arrays.append(array)

    def across(batch, y_steps, x_steps):
        halves = [(y_step, half) for y_step in y_steps for half in range(2)]
        add(batch, [(0, *entry) for entry in halves])
        for x_step in x_steps:
            moved = cycled(batch, "x", -x_step)
            add(moved, [(x_step, *entry) for entry in halves])

    above = cycled(own, "y", 1)
    below = cycled(own, "y", -1)
    across(own, (0,), (1, 3, 2))
    sides = jnp.concatenate([above, below])
    across(sides, (3, 1), (1, 3))
    early = len(arrays)
    opposite = cycled(own, "y", 2)
    across(opposite, (2,), (1, 3, 2))
    right, left = arrays[early - 2 : early]
    for moved, x_shift, y_step in ((left[:2], 1, 3), (right[2:], -1, 1)):
        moved = cycled(moved, "x", x_shift)
        add(moved, [(2, y_step, 0), (2, y_step, 1)])
    return arrays, pieces, early


CONTRACT_ROWS = (((0,), (0,)), ((), ()))
CONTRACT_COLS = (((1,), (1,)), ((), ()))
BLOCK = 256


def turned(values, cosine, sine_signed):
    return values * cosine + pltpu.roll(values, HEAD_DIM // 2, 1) * sine_signed


def unturned(values, cosine, sine_signed):
    return values * cosine - pltpu.roll(values, HEAD_DIM // 2, 1) * sine_signed


def accumulated(pieces, columns, place_ref, weights_ref, arrays, total, begun=None):
    first, last = columns
    for number, (array, at, x_step, y_step, half) in enumerate(pieces):
        place = place_ref[x_step * 4 + y_step]
        weight = weights_ref[(place // 2) * CORES + half, place % 2, :, first:last]
        term = lax.dot_general(
            arrays[array][at], weight, CONTRACT_ROWS, preferred_element_type=jnp.float32
        )
        if number == 0:
            total[...] = term if begun is None else begun[...] + term
        else:
            total[...] += term


def partial_kernel(pieces, columns, place_ref, weights_ref, cos_ref, sin_ref, *refs):
    *arrays, out_ref, total = refs
    accumulated(pieces, columns, place_ref, weights_ref, arrays, total)
    out_ref[...] = total[...]


def key_value_kernel(pieces, columns, place_ref, weights_ref, cos_ref, sin_ref, *refs):
    *arrays, begun, out_ref, total = refs
    accumulated(pieces, columns, place_ref, weights_ref, arrays, total, begun)
    keys = turned(total[:, :HEAD_DIM], cos_ref[...], sin_ref[...])
    out_ref[0] = keys.astype(jnp.bfloat16)
    out_ref[1] = total[:, HEAD_DIM:].astype(jnp.bfloat16)


def query_kernel(pieces, columns, place_ref, weights_ref, cos_ref, sin_ref, *refs, scale):
    *arrays, out_ref, total = refs
    accumulated(pieces, columns, place_ref, weights_ref, arrays, total)
    for head in range((columns[1] - columns[0]) // HEAD_DIM):
        part = total[:, head * HEAD_DIM : (head + 1) * HEAD_DIM]
        queries = turned(part, cos_ref[...], sin_ref[...]) * scale
        out_ref[:, head * HEAD_DIM : (head + 1) * HEAD_DIM] = queries.astype(jnp.bfloat16)


def attention_kernel(low_ref, q_ref, far_ref, near_ref, own_ref, grad_ref, att_ref, *refs):
    far_out, near_out, own_out, keys, values, acc = refs
    tokens, width = q_ref.shape
    for number, ref in enumerate((far_ref, near_ref, own_ref)):
        keys[number * tokens : (number + 1) * tokens] = ref[0]
        values[number * tokens : (number + 1) * tokens] = ref[1]
    acc[...] = jnp.zeros_like(acc)
    span = 2 * tokens + BLOCK
    heads = width // HEAD_DIM
    for head in range(heads):
        cols = slice(head * HEAD_DIM, (head + 1) * HEAD_DIM)
        for at in range(0, tokens, BLOCK):
            rows = slice(at, at + BLOCK)
            window = slice(at, at + span)
            low = low_ref[:, rows]
            key_at = lax.broadcasted_iota(jnp.int32, (span, BLOCK), 0) + at
            query_at = lax.broadcasted_iota(jnp.int32, (span, BLOCK), 1) + (2 * tokens + at)
            allowed = (key_at >= low) & (key_at <= query_at)
            query = q_ref[rows, cols]
            grad = grad_ref[rows, cols]
            scores = lax.dot_general(
                keys[window], query, CONTRACT_COLS, preferred_element_type=jnp.float32
            )
            scores = jnp.where(allowed, scores, -jnp.inf)
            raw = jnp.exp(scores - jnp.max(scores, axis=0, keepdims=True))
            probs = raw * (1.0 / jnp.sum(raw, axis=0, keepdims=True))
            low_probs = probs.astype(jnp.bfloat16)
            attended = lax.dot_general(
                values[window], low_probs, CONTRACT_ROWS, preferred_element_type=jnp.float32
            )
            attended = attended.T.astype(jnp.bfloat16)
            att_ref[rows, cols] = attended
            product = grad.astype(jnp.float32) * attended.astype(jnp.float32)
            out_dot = jnp.sum(product.T, axis=0, keepdims=True)
            acc[1, window] += jnp.dot(low_probs, grad, preferred_element_type=jnp.float32)
            prob_grad = lax.dot_general(
                values[window], grad, CONTRACT_COLS, preferred_element_type=jnp.float32
            )
            score_grad = (probs * (prob_grad - out_dot)).astype(jnp.bfloat16)
            acc[0, window] += jnp.dot(score_grad, query, preferred_element_type=jnp.float32)
    far_out[...] = acc[:, :tokens].astype(jnp.bfloat16)
    near_out[...] = acc[:, tokens : 2 * tokens].astype(jnp.bfloat16)
    own_out[...] = acc[:, 2 * tokens :]


def attention_call(low, queries, far, near, own, grads):
    tokens, width = queries.shape
    vmem = pl.BlockSpec(memory_space=pltpu.VMEM)
    block = jax.ShapeDtypeStruct(own.shape, jnp.bfloat16)
    pairs = tokens * (2 * tokens + BLOCK) * (width // HEAD_DIM)
    return pl.pallas_call(
        attention_kernel,
        out_shape=(
            jax.ShapeDtypeStruct((tokens, width), jnp.bfloat16),
            block,
            block,
            jax.ShapeDtypeStruct(own.shape, jnp.float32),
        ),
        in_specs=[vmem] * 6,
        out_specs=(vmem,) * 4,
        scratch_shapes=[
            pltpu.VMEM((3 * tokens, HEAD_DIM), jnp.bfloat16),
            pltpu.VMEM((3 * tokens, HEAD_DIM), jnp.bfloat16),
            pltpu.VMEM((2, 3 * tokens, HEAD_DIM), jnp.float32),
        ],
        compiler_params=pltpu.CompilerParams(vmem_limit_bytes=10 << 20),
        cost_estimate=pl.CostEstimate(
            flops=10 * pairs * HEAD_DIM,
            bytes_accessed=4 * tokens * width * 4,
            transcendentals=pairs,
        ),
        name="attention",
    )(low, queries, far, near, own, grads)


def chosen_kernel(place_ref, first_ref, second_ref, out_ref):
    out_ref[...] = jnp.where(place_ref[16] == 0, first_ref[...], second_ref[...])


def joined_kernel(place_ref, far_ref, near_ref, out_ref):
    near = jnp.where(place_ref[16] == 0, 0.0, near_ref[...].astype(jnp.float32))
    out_ref[...] = (far_ref[...].astype(jnp.float32) + near).astype(jnp.bfloat16)


def on_small_block(kernel, place, first, second):
    vmem = pl.BlockSpec(memory_space=pltpu.VMEM)
    return pl.pallas_call(
        kernel,
        out_shape=jax.ShapeDtypeStruct(first.shape, first.dtype),
        in_specs=[pl.BlockSpec(memory_space=pltpu.SMEM), vmem, vmem],
        out_specs=vmem,
        compiler_params=pltpu.CompilerParams(vmem_limit_bytes=10 << 20),
        cost_estimate=pl.CostEstimate(
            flops=first.size, bytes_accessed=6 * first.size, transcendentals=0
        ),
        name="small_block",
    )(place, first, second)


def project(kernel, out_shape, arrays, pieces, columns, place, weights, tables, begun=()):
    tokens = arrays[0].shape[2]
    width = columns[1] - columns[0]
    depth = len(pieces) * arrays[0].shape[1]
    vmem = pl.BlockSpec(memory_space=pltpu.VMEM)
    return pl.pallas_call(
        functools.partial(kernel, pieces, columns),
        out_shape=out_shape,
        in_specs=[pl.BlockSpec(memory_space=pltpu.SMEM)] + [vmem] * (3 + len(arrays) + len(begun)),
        out_specs=vmem,
        scratch_shapes=[pltpu.VMEM((tokens, width), jnp.float32)],
        compiler_params=pltpu.CompilerParams(vmem_limit_bytes=10 << 20),
        cost_estimate=pl.CostEstimate(
            flops=2 * tokens * depth * width,
            bytes_accessed=2 * depth * (tokens + width) + 4 * tokens * width,
            transcendentals=0,
        ),
        name="project",
    )(place, weights, *tables, *arrays, *begun)


def weight_grad_kernel(
    pieces, partner, place_ref, own_ref, near_ref, far_ref, cos_ref, sin_ref, *refs
):
    *arrays, out_ref, grads = refs
    core = place_ref[16]
    wanted = 1 - core if partner else core
    sums = [
        own_ref[i]
        + jnp.where(core == 0, near_ref[i].astype(jnp.float32), 0.0)
        + far_ref[i].astype(jnp.float32)
        for i in range(2)
    ]
    grads[:, :HEAD_DIM] = unturned(sums[0], cos_ref[...], sin_ref[...]).astype(jnp.bfloat16)
    grads[:, HEAD_DIM:] = sums[1].astype(jnp.bfloat16)
    for array, at, x_step, y_step, half in pieces:
        if half == 0:
            term = jnp.dot(
                arrays[array][at + wanted], grads[...], preferred_element_type=jnp.float32
            )
            out_ref[place_ref[x_step * 4 + y_step]] = term.astype(jnp.bfloat16)


def weight_grad(arrays, pieces, place, own, near, far, tables, partner):
    rows, tokens = arrays[0].shape[1:]
    width = 2 * HEAD_DIM
    vmem = pl.BlockSpec(memory_space=pltpu.VMEM)
    depth = len(pieces) * rows // 2
    return pl.pallas_call(
        functools.partial(weight_grad_kernel, pieces, partner),
        out_shape=jax.ShapeDtypeStruct((16, rows, width), jnp.bfloat16),
        in_specs=[pl.BlockSpec(memory_space=pltpu.SMEM)] + [vmem] * (5 + len(arrays)),
        out_specs=vmem,
        scratch_shapes=[pltpu.VMEM((tokens, width), jnp.bfloat16)],
        compiler_params=pltpu.CompilerParams(vmem_limit_bytes=10 << 20),
        cost_estimate=pl.CostEstimate(
            flops=2 * tokens * depth * width,
            bytes_accessed=2 * depth * (tokens + width) + 2 * tokens * width,
            transcendentals=0,
        ),
        name="weight_grad",
    )(place, own, near, far, *tables, *arrays)


def scattered_sum(kept, sent):
    chip = kept.astype(jnp.float32) + cycled(sent, "core", 1).astype(jnp.float32)
    chip = chip.astype(jnp.bfloat16)
    landed = lax.all_to_all(chip, ("z", "far"), 0, 0, tiled=True)
    return jnp.sum(landed.astype(jnp.float32), axis=0)


def spread_weights(query_weight, key_weight, value_weight):
    own = jnp.concatenate([query_weight, key_weight, value_weight], axis=1)
    other = cycled(own, "far", 1)
    far = lax.axis_index("far")
    both = jnp.where(far == 0, jnp.stack([own, other]), jnp.stack([other, own]))
    return lax.all_gather(both, ("z", "core"), axis=0, tiled=False)


def shards(features, query_weight, key_weight, value_weight, doc_lengths, out_grad):
    tok_rows, slab_rows = features.shape
    query_cols = query_weight.shape[1]
    value_cols = key_weight.shape[1]
    query_scale = (slab_rows * 16 / HEADS_Q) ** (-0.5)
    ctx_index = lax.axis_index(CTX)

    arrays, pieces, early = spread_features(features.T.reshape(2, slab_rows // 2, tok_rows))
    weights = spread_weights(query_weight, key_weight, value_weight)
    step = jnp.arange(4, dtype=jnp.int32)
    x_at, y_at = lax.axis_index("x"), lax.axis_index("y")
    place = ((x_at + step) % 4)[:, None] * 4 + ((y_at + step) % 4)[None, :]
    place = jnp.concatenate([place.reshape(16), jnp.stack([lax.axis_index("core"), y_at])])
    place = place.astype(jnp.int32)

    starts = jnp.cumsum(doc_lengths) - doc_lengths
    query_index = ctx_index * tok_rows + jnp.arange(tok_rows, dtype=jnp.int32)
    query_start = start_of(query_index, starts)
    tables = rope_tables(query_index - query_start)
    low = jnp.maximum(query_start, query_index - (WINDOW - 1)) - (ctx_index - SPAN) * tok_rows
    low, tables = lax.optimization_barrier((low.astype(jnp.int32)[None], tables))

    columns = (query_cols, query_cols + 2 * value_cols)
    begun = project(
        partial_kernel,
        jax.ShapeDtypeStruct((tok_rows, 2 * value_cols), jnp.float32),
        arrays[:early],
        [piece for piece in pieces if piece[0] < early],
        columns,
        place,
        weights,
        tables,
    )
    key_value = project(
        key_value_kernel,
        jax.ShapeDtypeStruct((2, tok_rows, HEAD_DIM), jnp.bfloat16),
        arrays[early:],
        [(piece[0] - early, *piece[1:]) for piece in pieces if piece[0] >= early],
        columns,
        place,
        weights,
        tables,
        (begun,),
    )
    far = passed_along(key_value, CORES)
    near = cycled(on_small_block(chosen_kernel, place, key_value, far), "core", 1)
    queries = project(
        functools.partial(query_kernel, scale=query_scale),
        jax.ShapeDtypeStruct((tok_rows, query_cols), jnp.bfloat16),
        arrays,
        pieces,
        (0, query_cols),
        place,
        weights,
        tables,
    )
    attention, far_part, near_part, own_part = attention_call(
        low, queries, far, near, key_value, out_grad
    )
    near_back = cycled(near_part, "core", 1)
    far_back = passed_along(on_small_block(joined_kernel, place, far_part, near_back), -CORES)
    sent, kept = (
        weight_grad(arrays, pieces, place, own_part, near_back, far_back, tables, partner)
        for partner in (True, False)
    )
    weight_grads = scattered_sum(kept, sent).astype(jnp.bfloat16)
    return attention, weight_grads[:, :value_cols], weight_grads[:, value_cols:]


def solution(mesh):
    sizes = (mesh.shape["ctx"] // 4, 2, 2, 4, 4)
    torus = Mesh(mesh.devices.reshape(sizes), CTX + HEAD)
    placed = (P(CTX, HEAD), P(CTX, HEAD), P(CTX, HEAD), P(CTX, HEAD), P(), P(CTX, HEAD))
    return jax.shard_map(
        shards,
        mesh=torus,
        in_specs=placed,
        out_specs=(P(CTX, HEAD), P(CTX, HEAD), P(CTX, HEAD)),
        check_vma=False,
    )
```
